32 devices in a mesh: groups: 2 (over x), ctx: 16 (over z, y, core).
Axes of the slice: x: 2, y: 2, z: 4, core: 2. Of those that a mesh axis runs over, the one named last changes fastest.
Arguments:
- inputs: bfloat16 [4096, 8192], P(None, ('groups', 'ctx')), parts along dimension 1, may hold values from -4 to 4
- projections: bfloat16 [512, 8192], P(None, ('groups', 'ctx')), parts along dimension 1, may hold values from -7 to 7
- step_sizes: bfloat16 [64, 8192], P(None, ('groups', 'ctx')), parts along dimension 1, may hold values from 0.0019989014 to 0.019897461
- log_rates: float32 [64], replicated, may hold values from -12 to 3
- skip_gain: float32 [64], replicated, may hold values from 0.5 to 1.5
- packing: int32 [32, 256], P(('groups', 'ctx')), parts along dimension 0, may hold values from 0 to 255, as said below
- prompt_sizes: int32 [8], P('groups'), parts along dimension 0, may hold values from 1 to 3072, 4096 in all
Outputs:
- ssd_output: bfloat16 [4096, 8192], P(None, ('groups', 'ctx')), parts along dimension 1
The draws below stay inside these ranges and needn't reach their ends.
There are 2 independent parts, one for each index of `groups`. The reference program is written for one: setup_inputs(seed, part) draws one part's arguments, and reference() takes and returns one part's arrays. A program takes and returns all parts, laid end to end along the dimension named above; an argument that names none is the same for every part. Nothing has to cross between parts.
Inputs may be any that keep to these rules, and one draw needn't show every extreme that they name: `packing`: each row names every one of the loader's 256 tokens once. `prompt_sizes`: the lengths add up to 4096.
All inputs are finite; a program needn't handle non-finite values.
Results may differ from the reference program's by a relative error of at most 0.001.
The reference program's roundings to bfloat16 on the way count: a program that leaves them out, or rounds other values in their place, can miss the bound.
Values may be sent and summed in bfloat16 or wider, within the bound.
A program may use at most 320 MiB of HBM per device.

```python
import math
import jax
import jax.numpy as jnp
import numpy as np
from jax import lax

H = 64
G = 4
P_SIZE = 64
N = 64
BLOCK = 128
NSEQ = 4
TOK_DEV = 256
TOKENS = 4096
SLOT = 16
N_CTX = 16


def make_order(row_key):
    return jax.random.permutation(row_key, TOK_DEV)


def loader_plan(key):
    row_keys = jax.random.split(jax.random.fold_in(key, 7), N_CTX)
    return jax.vmap(make_order)(row_keys).astype(jnp.int32)


def owner_profile(key):
    loader_order = loader_plan(key)
    slot_width = TOK_DEV // N_CTX
    handed = jnp.broadcast_to(jnp.arange(TOK_DEV, dtype=jnp.int32) // slot_width, (N_CTX, TOK_DEV))
    loader_ids = jnp.broadcast_to(jnp.arange(N_CTX, dtype=jnp.int32)[:, None], (N_CTX, TOK_DEV))
    owners = jnp.zeros((N_CTX, TOK_DEV), jnp.int32).at[loader_ids, loader_order].set(handed).reshape(-1)
    phase_shift = jax.random.randint(jax.random.fold_in(key, 3), (), 0, 8)
    shifted = owners + 8 - phase_shift
    offset = shifted % 8
    pair_signs = (2 * jax.random.randint(jax.random.fold_in(key, 5), (N_CTX // 8 + 2,), 0, 2) - 1).astype(jnp.float32)
    polarity = pair_signs[shifted // 8] * jnp.where(offset == 0, 1.0, -1.0)
    loud_mask = offset < 2
    return (loud_mask, polarity)


def draw_jitter(jitter_key, shape_full):
    jitter = jax.random.truncated_normal(jitter_key, -4.0, 4.0, shape_full, jnp.float32)
    return jitter


def draw_packing(key, part):
    return loader_plan(key)


def draw_inputs(key, part):
    loud_mask, polarity = owner_profile(key)
    jitter_key, mean_key, sign_key = jax.random.split(jax.random.fold_in(key, 21), 3)
    jitter = draw_jitter(jitter_key, (H * P_SIZE, TOKENS))
    magnitude = jax.random.uniform(mean_key, (H * P_SIZE,), jnp.float32, 0.5, 1.0)
    channel_sign = (2 * jax.random.randint(sign_key, (H * P_SIZE,), 0, 2) - 1).astype(jnp.float32)
    common_level = (magnitude * channel_sign)[:, None] * polarity[None, :]
    return jnp.where(loud_mask[None, :], common_level + 0.5 * jitter, jitter).astype(jnp.bfloat16)


def draw_projections(key, part):
    loud_mask, polarity = owner_profile(key)
    jitter = draw_jitter(jax.random.fold_in(key, 31), (G * 2 * N, TOKENS))
    common_level = (0.38 / N) ** 0.5
    row_index = jnp.arange(G * 2 * N, dtype=jnp.int32)
    input_rows = (row_index // N % 2 == 0)[:, None]
    loud_cols = loud_mask[None, :]
    input_map = jnp.where(loud_cols, 5.0 * (common_level + 0.15 * jitter), 0.06 * jitter)
    output_map = jnp.where(loud_cols, 0.2 * (common_level + 0.3 * jitter), 5.0 * (common_level + 0.3 * jitter))
    return jnp.where(input_rows, input_map, output_map).astype(jnp.bfloat16)


def draw_log_rates(key, part):
    order_key, slow_key, mid_key, fast_key = jax.random.split(key, 4)
    head_rank = jax.random.permutation(order_key, H)
    fast_count = H // 4
    mid_count = H // 4
    slow_vals = jax.random.uniform(slow_key, (H,), jnp.float32, jnp.log(0.2), jnp.log(2.3)) - jnp.log(0.0078 * TOKENS)
    mid_vals = jax.random.uniform(mid_key, (H,), jnp.float32, jnp.log(0.36), jnp.log(2.3)) - jnp.log(0.0078 * TOK_DEV)
    fast_vals = jax.random.uniform(fast_key, (H,), jnp.float32, jnp.log(3.0), jnp.log(12.0))
    picked = jnp.where(head_rank < fast_count, fast_vals, jnp.where(head_rank < fast_count + mid_count, mid_vals, slow_vals))
    return picked.astype(jnp.float32)


def block_levels(rng, dims, cuts, least, top_value):
    def one(dim, shards_of):
        steps = jax.random.uniform(jax.random.fold_in(jax.random.fold_in(rng, 6), dim), (shards_of,), jnp.float32, least / len(cuts), top_value / len(cuts))
        return jnp.repeat(jnp.exp(steps), dims[dim] // shards_of).reshape((-1,) + (1,) * (len(dims) - dim - 1))

    loudness = one(*cuts[0])
    for cut in cuts[1:]:
        loudness = loudness * one(*cut)
    return loudness


def length_profile(amount, total, bound, skew):
    weights = [(1 << 20) // math.isqrt(rank ** skew) + 1 for rank in range(2, amount + 1)]
    rest, counts = total - bound - (amount - 1), [1] * (amount - 1)
    while rest > 0:
        movable = [i for i in range(amount - 1) if counts[i] < bound]
        pool, budget = sum([weights[i] for i in movable]), rest
        for i in movable:
            extra = min(bound - counts[i], max(1, budget * weights[i] // pool), rest)
            counts[i] = counts[i] + extra
            rest = rest - extra
    return np.array([bound] + counts)


def ragged_sizes(own_key, count, total, most, lean):
    if count == 2:
        one = jax.random.randint(own_key, (), max(1, total - most), min(most, total - 1) + 1)
        return jnp.stack([one, total - one])
    lengths = jnp.asarray(length_profile(count, total, most, lean), jnp.int32)
    pairs = (count - 1) // 2
    donor, sink = lengths[1:1 + 2 * pairs:2], lengths[2:2 + 2 * pairs:2]
    slack = jnp.minimum(donor - 1, most - sink)
    moved = jax.random.randint(jax.random.fold_in(own_key, 1), (pairs,), 0, 1 << 20) % (slack + 1)
    lengths = lengths.at[1:1 + 2 * pairs:2].set(donor - moved).at[2:2 + 2 * pairs:2].set(sink + moved)
    return lengths[jax.random.permutation(jax.random.fold_in(own_key, 2), count)]


def setup_inputs(seed: int = 0, part: int = 0) -> dict:
    keys = jax.random.split(jax.random.key(seed), 8)
    part_keys = jax.random.split(jax.random.fold_in(keys[7], part), 8)
    return {
        "inputs": draw_inputs(jax.random.fold_in(jax.random.fold_in(keys[7], part), 71), part),
        "projections": draw_projections(jax.random.fold_in(jax.random.fold_in(keys[7], part), 71), part),
        "step_sizes": jnp.clip(jnp.exp(math.log(0.019897461) - 2.2979944 * jax.random.uniform(part_keys[2], (H, TOKENS), jnp.float32) ** block_levels(part_keys[2], (H, TOKENS), ((1, 16),), -0.2, 0.2)), 0.0019989014, 0.019897461).astype(jnp.bfloat16),
        "log_rates": draw_log_rates(jax.random.fold_in(keys[7], 71), part),
        "skip_gain": jnp.clip(jax.random.uniform(keys[4], (H,), jnp.float32, 0.5, 1.5), 0.5, 1.5),
        "packing": draw_packing(jax.random.fold_in(jax.random.fold_in(keys[7], part), 71), part),
        "prompt_sizes": ragged_sizes(part_keys[6], NSEQ, TOKENS, TOKENS * 3 // 4, 2).astype(jnp.int32),
    }


def rounded(value):
    return lax.optimization_barrier(value.astype(jnp.bfloat16)).astype(jnp.float32)


def block_result(block_x, block_bc, block_dt, segment, resets, decay_rate, skip_gain, carry_in):
    length = block_x.shape[1]
    per_group = H // G
    exact = lax.Precision.HIGHEST
    x_heads = block_x.astype(jnp.float32).reshape(G, per_group, P_SIZE, length)
    maps = block_bc.astype(jnp.float32).reshape(G, 2, N, length)
    input_map = maps[:, 0]
    output_map = maps[:, 1]
    step_size = block_dt.astype(jnp.float32)
    log_decay = jnp.cumsum(step_size * decay_rate[:, None], axis=1)
    before_reset = jnp.cumsum(resets) == 0
    column_index = jnp.arange(length, dtype=jnp.int32)
    allowed = (column_index[:, None] >= column_index[None, :]) & (segment[:, None] == segment[None, :])
    decay_gap = log_decay[:, :, None] - log_decay[:, None, :]
    decay_mask = jnp.exp(jnp.where(allowed[None], decay_gap, -jnp.inf))
    scaled_mask = (decay_mask * step_size[:, None, :]).reshape(G, per_group, length, length)
    inner_gram = jnp.einsum("gni,gnj->gij", output_map, input_map, precision=exact)
    mixing = rounded(inner_gram[:, None] * scaled_mask)
    within = jnp.einsum("ghij,ghpj->ghpi", mixing, x_heads, precision=exact)
    opened = jnp.where(before_reset[None, :], jnp.exp(log_decay), jnp.float32(0.0)).reshape(G, per_group, 1, length)
    carried = jnp.einsum("ghpn,gni->ghpi", rounded(carry_in).reshape(G, per_group, P_SIZE, N), output_map, precision=exact)
    result = within + carried * opened + skip_gain.reshape(G, per_group, 1, 1) * x_heads
    last_decay = log_decay[:, -1:]
    into_end = jnp.where((segment == segment[-1])[None, :], jnp.exp(last_decay - log_decay), jnp.float32(0.0)) * step_size
    weighted = rounded(x_heads * into_end.reshape(G, per_group, 1, length))
    block_total = jnp.einsum("ghpj,gnj->ghpn", weighted, input_map, precision=exact).reshape(H, P_SIZE, N)
    block_keep = jnp.where(before_reset[-1], jnp.exp(last_decay[:, 0]), jnp.float32(0.0))
    next_state = block_keep[:, None, None] * carry_in + block_total
    return next_state, result.reshape(-1, length).astype(jnp.bfloat16)


def reference(inputs, projections, step_sizes, log_rates, skip_gain, packing, prompt_sizes):
    loader_base = (jnp.arange(N_CTX, dtype=jnp.int32) * TOK_DEV)[:, None, None]
    source = (packing.reshape(N_CTX, N_CTX, SLOT) + loader_base).transpose(1, 0, 2).reshape(-1).astype(jnp.int32)
    ordered_x = jnp.take(inputs, source, axis=1)
    ordered_bc = jnp.take(projections, source, axis=1)
    ordered_dt = jnp.take(step_sizes, source, axis=1)
    prompt_start = (jnp.cumsum(prompt_sizes) - prompt_sizes).astype(jnp.int32)
    decay_rate = -jnp.exp(log_rates)

    def advance(carry_in, first_col):
        position = first_col + jnp.arange(BLOCK, dtype=jnp.int32)
        segment = jnp.sum((position[:, None] >= prompt_start[None, :]).astype(jnp.int32), axis=1) - 1
        resets = jnp.sum((position[:, None] == prompt_start[None, :]).astype(jnp.int32), axis=1)
        block_x = lax.dynamic_slice_in_dim(ordered_x, first_col, BLOCK, 1)
        block_bc = lax.dynamic_slice_in_dim(ordered_bc, first_col, BLOCK, 1)
        block_dt = lax.dynamic_slice_in_dim(ordered_dt, first_col, BLOCK, 1)
        return block_result(block_x, block_bc, block_dt, segment, resets, decay_rate, skip_gain, carry_in)

    first_cols = jnp.arange(TOKENS // BLOCK, dtype=jnp.int32) * BLOCK
    zero_state = jnp.zeros((H, P_SIZE, N), jnp.float32)
    final_state, blocks_out = lax.scan(advance, zero_state, first_cols)
    return blocks_out.transpose(1, 0, 2).reshape(H * P_SIZE, TOKENS)
```

```python
import functools
import jax
import jax.numpy as jnp
from jax import lax
from jax.experimental import pallas as pl
from jax.experimental.pallas import tpu as pltpu
from jax.sharding import PartitionSpec as P

G = 4
BLOCK = 128
LANES = 128
PLANE = 4
MAX_LAG = 3
VLIM = 36 * 1024 * 1024
F32 = jnp.float32
BF16 = jnp.bfloat16
MESH = pl.DeviceIdType.MESH


def dot_nt(a, b):
    return lax.dot_general(a, b, (((1,), (1,)), ((), ())), preferred_element_type=F32)


def starts_of(sizes_ref):
    out = []
    at = jnp.int32(0)
    for s in range(sizes_ref.shape[0]):
        out.append(at)
        at = at + sizes_ref[s]
    return out


def segment_of(position, starts):
    seg = jnp.zeros(position.shape, jnp.int32)
    for at in starts:
        seg = seg + (position >= at).astype(jnp.int32)
    return seg


def decay_of(dt, rate):
    t = dt.shape[0]
    tri = jnp.where(
        lax.broadcasted_iota(jnp.int32, (t, t), 0) >= lax.broadcasted_iota(jnp.int32, (t, t), 1),
        1.0, 0.0).astype(F32)
    return jnp.dot(tri, dt * rate, preferred_element_type=F32, precision=lax.Precision.HIGHEST)


def spread(value, heads, width):
    rows = value.shape[0]
    per = LANES // width
    lane = lax.broadcasted_iota(jnp.int32, (rows, LANES), 1)
    out = []
    for q in range(heads // per):
        acc = jnp.broadcast_to(value[:, q * per:q * per + 1], (rows, LANES))
        for k in range(1, per):
            other = jnp.broadcast_to(value[:, q * per + k:q * per + k + 1], (rows, LANES))
            acc = jnp.where(lane >= k * width, other, acc)
        out.append(acc)
    return jnp.concatenate(out, axis=1)


def fused_kernel(
    n, heads, width, states, window,
    sizes_hbm, skip_hbm, rate_hbm, pack_hbm, x_hbm, bc_hbm, dt_hbm, o_hbm,
    sizes_ref, skip_ref, rate_ref, pack_ref, dt_ref,
    xv, bv, pick, ys, yr, ds, dr,
    cum_g, into_g, keep_g, cum_t, dt_t, opens, maps_t, gram, allow, acc, obuf,
    t_own, t0, t_in, enter, leave, out_e, carry,
    in_sem, few_sem, out_sem, ds_sem, dr_sem, ys_sem, yr_sem,
    ts_sem, tr_sem, es_sem, er_sem, cs_sem, cr_sem,
):
    me = lax.axis_index("ctx")
    tok = dt_ref.shape[1]
    slot = tok // n
    part = heads // 2
    wp = part * width
    wx = heads * width
    wm = 2 * states
    wq = wp // PLANE
    chunks = 2 * G
    blocks = tok // BLOCK
    half = n // 2
    q = lax.rem(me, PLANE)
    z = me // PLANE
    nz = n // PLANE
    base = me * tok
    lag = jnp.minimum(z, MAX_LAG)

    def loop(count, body, low=0):
        def step(i, _):
            body(i)
            return 0
        lax.fori_loop(low, count, step, 0)

    barrier = pltpu.get_barrier_semaphore()
    loop(n, lambda off: pl.semaphore_signal(
        barrier, inc=1, device_id={"ctx": lax.rem(me + off, n)}, device_id_type=MESH), low=1)

    def load_x(c):
        r = pl.ds(pl.multiple_of(c * wp, LANES), wp)
        return pltpu.make_async_copy(x_hbm.at[r], xv.at[c], in_sem.at[0, c])

    def load_m(g):
        r = pl.ds(pl.multiple_of(g * wm, LANES), wm)
        return pltpu.make_async_copy(bc_hbm.at[r], bv.at[g], in_sem.at[1, g])

    few = [
        pltpu.make_async_copy(src, dst, few_sem.at[i])
        for i, (src, dst) in enumerate((
            (pack_hbm, pack_ref), (dt_hbm, dt_ref), (sizes_hbm, sizes_ref),
            (skip_hbm, skip_ref), (rate_hbm, rate_ref)))
    ]
    few[0].start()
    few[1].start()
    load_m(0).start()
    load_x(0).start()
    load_x(1).start()
    for copy in few[2:]:
        copy.start()
    loop(G, lambda g: load_m(g).start(), low=1)
    loop(chunks, lambda c: load_x(c).start(), low=2)
    few[0].wait()

    rows = lax.broadcasted_iota(jnp.int32, (tok, tok), 0)
    pick[...] = jnp.where(rows == pack_ref[...], 1.0, 0.0).astype(F32).T.astype(BF16)
    head_count = dt_ref.shape[0]
    few[1].wait()
    dt_all = dot_nt(pick[...], dt_ref[...]).astype(BF16)
    dt_all = jnp.concatenate([dt_all, jnp.zeros((tok, LANES - head_count), BF16)], axis=1)
    ds[...] = dt_all.reshape(n, slot, LANES)

    def lanes_of(k):
        return slice(0, wm + wp) if k == 0 else slice(wm + wp, wm + wx)

    def prep(g, k):
        if k == 0:
            load_m(g).wait()
            ys[g, :, :, :wm] = dot_nt(pick[...], bv[g]).astype(BF16).reshape(n, slot, wm)
        load_x(2 * g + k).wait()
        y = dot_nt(pick[...], xv[2 * g + k]).astype(BF16)
        ys[g, :, :, wm + k * wp:wm + (k + 1) * wp] = y.reshape(n, slot, wp)

    def send_y(g, k, off):
        to = lax.rem(me + off, n)
        s = lanes_of(k)
        return pltpu.make_async_remote_copy(
            ys.at[g, to, :, s], yr.at[g, me, :, s], ys_sem.at[g, k], yr_sem.at[g, k],
            device_id={"ctx": to}, device_id_type=MESH)

    def send_d(off):
        to = lax.rem(me + off, n)
        return pltpu.make_async_remote_copy(
            ds.at[to], dr.at[me], ds_sem.at[0], dr_sem.at[0],
            device_id={"ctx": to}, device_id_type=MESH)

    def spread_out(send):
        def pair(i):
            send(half - i).start()

            @pl.when(i > 0)
            def _():
                send(half + i).start()

        loop(half, pair)

    def issue(g, k):
        s = lanes_of(k)
        spread_out(lambda off: send_y(g, k, off))
        pltpu.make_async_copy(ys.at[g, me, :, s], yr.at[g, me, :, s], yr_sem.at[g, k]).start()

    def arrived(g, k):
        s = lanes_of(k)
        pltpu.make_async_copy(ys.at[g, :, :, s], yr.at[g, :, :, s], yr_sem.at[g, k]).wait()

    def departed(g, k):
        s = lanes_of(k)
        most = slice(0, n - 1)
        pltpu.make_async_copy(ys.at[g, most, :, s], yr.at[g, most, :, s], ys_sem.at[g, k]).wait()

    prep(0, 0)
    pl.semaphore_wait(barrier, n - 1)
    spread_out(send_d)
    pltpu.make_async_copy(ds.at[me], dr.at[me], dr_sem.at[0]).start()
    issue(0, 0)
    prep(0, 1)
    issue(0, 1)

    def prep_rest(g):
        prep(g, 0)
        prep(g, 1)

    loop(G, prep_rest, low=1)

    for copy in few[2:]:
        copy.wait()
    starts = starts_of(sizes_ref)
    rate = jnp.concatenate(
        [rate_ref[...], jnp.zeros((1, LANES - head_count), F32)], axis=1)
    rate = jnp.broadcast_to(-jnp.exp(rate), (8, LANES))[0:1]

    pltpu.make_async_copy(ds, dr, dr_sem.at[0]).wait()

    def rows_of(b):
        return slice(b * BLOCK // slot, (b + 1) * BLOCK // slot)

    for b in range(blocks):
        head = base + b * BLOCK
        last = head + BLOCK - 1
        dt = dr[rows_of(b)].reshape(BLOCK, LANES).astype(F32)
        cum = decay_of(dt, rate)
        end = cum[BLOCK - 1:BLOCK, :]
        pos = head + lax.broadcasted_iota(jnp.int32, (BLOCK, LANES), 0)
        last_seg = jnp.int32(0)
        cut = jnp.int32(0)
        for at in starts:
            last_seg = last_seg + (last >= at).astype(jnp.int32)
            cut = cut + ((at >= head) & (at <= last)).astype(jnp.int32)
        same = segment_of(pos, starts) == last_seg
        into = jnp.where(same, jnp.exp(end - cum), 0.0) * dt
        keep = jnp.broadcast_to(jnp.where(cut == 0, jnp.exp(end), 0.0), (8, LANES))
        for g in range(G):
            shift = (LANES - g * heads) % LANES
            cum_g[g, b] = pltpu.roll(cum, shift, 1)
            into_g[g, b] = pltpu.roll(into, shift, 1)
            keep_g[g, b] = pltpu.roll(keep, shift, 1)
        across = cum.T[:head_count]
        cum_t[b] = across
        dt_t[b] = dt.T[:head_count]
        row_pos = head + lax.broadcasted_iota(jnp.int32, (1, BLOCK), 1)
        row_cut = jnp.zeros((1, BLOCK), jnp.int32)
        for at in starts:
            row_cut = row_cut + ((row_pos >= at) & (at >= head)).astype(jnp.int32)
        opens[b] = jnp.where(row_cut == 0, jnp.exp(across), 0.0)
        pos_i = head + lax.broadcasted_iota(jnp.int32, (BLOCK, BLOCK), 0)
        pos_j = head + lax.broadcasted_iota(jnp.int32, (BLOCK, BLOCK), 1)
        fits = (pos_i >= pos_j) & (segment_of(pos_i, starts) == segment_of(pos_j, starts))
        allow[b] = jnp.where(fits, 0.0, -jnp.inf)

    def y_of(g, b, lo, hi):
        return yr[g, rows_of(b), :, lo:hi].reshape(BLOCK, hi - lo)

    def x_of(g, k, b):
        return y_of(g, b, wm + k * wp, wm + (k + 1) * wp)

    def quarter(k):
        return slice(k * wq, (k + 1) * wq)

    def send_total(c, hop):
        to = lax.rem(q + hop, PLANE)
        s = pl.ds(pl.multiple_of(to * wq, LANES), wq)
        return pltpu.make_async_remote_copy(
            t_own.at[c, :, s], t_in.at[c, q], ts_sem.at[c, hop], tr_sem.at[c, hop],
            device_id={"ctx": z * PLANE + to}, device_id_type=MESH)

    def own_total(c):
        s = pl.ds(pl.multiple_of(q * wq, LANES), wq)
        return pltpu.make_async_copy(t_own.at[c, :, s], t_in.at[c, q], tr_sem.at[c, 0])

    def send_leave(c):
        return pltpu.make_async_remote_copy(
            leave.at[c], enter.at[c], es_sem.at[c], er_sem.at[c],
            device_id={"ctx": me + PLANE}, device_id_type=MESH)

    def take_enter(c):
        return pltpu.make_async_remote_copy(
            leave.at[c], enter.at[c], es_sem.at[c], er_sem.at[c],
            device_id={"ctx": me - PLANE}, device_id_type=MESH)

    def send_entering(c, hop):
        to = lax.rem(q + hop, PLANE)
        return pltpu.make_async_remote_copy(
            out_e.at[c, to], carry.at[c, q], cs_sem.at[c, hop], cr_sem.at[c, hop],
            device_id={"ctx": z * PLANE + to}, device_id_type=MESH)

    def own_entering(c):
        return pltpu.make_async_copy(out_e.at[c, q], carry.at[c, q], cr_sem.at[c, 0])

    def states_stage(g, k):
        c = 2 * g + k
        total = None
        for b in range(blocks):
            if k == 0:
                in_map = y_of(g, b, 0, states)
                out_map = y_of(g, b, states, wm)
                maps_t[b] = in_map.astype(F32).T.astype(BF16)
                gram[b] = dot_nt(out_map, in_map)
            cols = slice(k * part, (k + 1) * part)
            into = spread(into_g[g, b][:, cols], part, width)
            weighted = (x_of(g, k, b).astype(F32) * into).astype(BF16)
            block_total = jnp.dot(maps_t[b], weighted, preferred_element_type=F32)
            keep = spread(keep_g[g, b][:, cols], part, width)
            if total is None:
                total, gain = block_total, keep
            else:
                total = keep[0:1] * total + block_total
                gain = gain * keep
            if b < blocks - 1:
                t0[c, b, :states, :] = block_total
                t0[c, b, states:, :] = keep
        t_own[c, :states, :] = total
        t_own[c, states:, :] = gain
        for hop in range(1, PLANE):
            send_total(c, hop).start()
        own_total(c).start()

    def inner_stage(g, k):
        c = 2 * g + k
        first = pl.multiple_of(c * part, part)
        for b in range(blocks):
            lo = b * BLOCK
            cum = cum_g[g, b]
            across = cum_t[b, pl.ds(first, part), :]
            dt = dt_t[b, pl.ds(first, part), :]
            x_fm = x_of(g, k, b).T
            for h in range(part):
                col = k * part + h
                gap = jnp.broadcast_to(cum[:, col:col + 1], (BLOCK, BLOCK)) - across[h:h + 1]
                mask = jnp.exp(gap + allow[b])
                mixing = (gram[b] * (mask * dt[h:h + 1])).astype(BF16)
                r = slice(h * width, (h + 1) * width)
                xh = x_fm[r]
                acc[c, r, lo:lo + BLOCK] = (
                    dot_nt(xh, mixing) + skip_ref[c * part + h] * xh.astype(F32))

    def chain_stage(c):
        for hop in range(1, PLANE):
            send_total(c, hop).wait_recv()
        own_total(c).wait()

        @pl.when(z > 0)
        def _():
            take_enter(c).wait_recv()

        @pl.when(z == 0)
        def _():
            enter[c] = jnp.zeros((states, wq), F32)

        state = enter[c]
        for k in range(PLANE):
            out_e[c, k] = state
            state = t_in[c, k, states:states + 1, :] * state + t_in[c, k, :states, :]

        @pl.when(z < nz - 1)
        def _():
            leave[c] = state
            send_leave(c).start()

        for hop in range(1, PLANE):
            send_entering(c, hop).start()
        own_entering(c).start()

    def store_out(c):
        return pltpu.make_async_copy(
            obuf.at[c], o_hbm.at[pl.ds(pl.multiple_of(c * wp, LANES), wp)], out_sem.at[c])

    def output_stage(c):
        for hop in range(1, PLANE):
            send_entering(c, hop).wait_recv()
        own_entering(c).wait()
        g = c // 2
        first = pl.multiple_of(c * part, part)
        state = jnp.concatenate([carry[c, k] for k in range(PLANE)], axis=1)
        for b in range(blocks):
            lo = b * BLOCK
            out_map = y_of(g, b, states, wm)
            carried = dot_nt(state.astype(BF16).T, out_map)
            opened = opens[b, pl.ds(first, part), :]
            for h in range(part):
                r = slice(h * width, (h + 1) * width)
                obuf[c, r, lo:lo + BLOCK] = (
                    acc[c, r, lo:lo + BLOCK] + carried[r] * opened[h:h + 1]).astype(BF16)
            if b < blocks - 1:
                state = t0[c, b, states:states + 1, :] * state + t0[c, b, :states, :]
        store_out(c).start()

    def follow(step):
        c = step - lag

        @pl.when((c >= 0) & (c < chunks))
        def _():
            chain_stage(c)

        @pl.when((c >= 1) & (c <= chunks))
        def _():
            output_stage(c - 1)

    def turn(g):
        for k in range(2):
            arrived(g, k)

            @pl.when(g < G - 1)
            def _():
                issue(g + 1, k)

            states_stage(g, k)
            inner_stage(g, k)
            follow(2 * g + k)

    loop(G, turn)
    loop(chunks + lag + 1, follow, low=chunks)

    most = slice(0, n - 1)
    pltpu.make_async_copy(ds.at[most], dr.at[most], ds_sem.at[0]).wait()

    def close(g):
        for k in range(2):
            departed(g, k)
            c = 2 * g + k
            for hop in range(1, PLANE):
                send_total(c, hop).wait_send()
                send_entering(c, hop).wait_send()

            @pl.when(z < nz - 1)
            def _():
                send_leave(c).wait_send()

            store_out(c).wait()

    loop(G, close)


def per_device(n, inputs, projections, step_sizes, log_rates, skip_gain, packing, prompt_sizes):
    tok = inputs.shape[1]
    head_count = log_rates.shape[0]
    heads = head_count // G
    states = projections.shape[0] // (2 * G)
    width = inputs.shape[0] // head_count
    part = heads // 2
    wp = part * width
    wx = heads * width
    wm = 2 * states
    wq = wp // PLANE
    slot = tok // n
    blocks = tok // BLOCK
    rows = states + 8
    chunks = 2 * G
    hbm = pl.BlockSpec(memory_space=pltpu.HBM)
    dma = pltpu.SemaphoreType.DMA
    return pl.pallas_call(
        functools.partial(fused_kernel, n, heads, width, states, 2),
        in_specs=[hbm] * 7,
        out_specs=pl.BlockSpec(memory_space=pl.ANY),
        out_shape=jax.ShapeDtypeStruct((G * wx, tok), BF16),
        scratch_shapes=[
            pltpu.SMEM(prompt_sizes.shape, jnp.int32),
            pltpu.SMEM(skip_gain.shape, F32),
            pltpu.VMEM((1, head_count), F32),
            pltpu.VMEM((1, tok), jnp.int32),
            pltpu.VMEM((head_count, tok), BF16),
            pltpu.VMEM((chunks, wp, tok), BF16),
            pltpu.VMEM((G, wm, tok), BF16),
            pltpu.VMEM((tok, tok), BF16),
            pltpu.VMEM((G, n, slot, wm + wx), BF16),
            pltpu.VMEM((G, n, slot, wm + wx), BF16),
            pltpu.VMEM((n, slot, LANES), BF16),
            pltpu.VMEM((n, slot, LANES), BF16),
            pltpu.VMEM((G, blocks, BLOCK, LANES), F32),
            pltpu.VMEM((G, blocks, BLOCK, LANES), F32),
            pltpu.VMEM((G, blocks, 8, LANES), F32),
            pltpu.VMEM((blocks, head_count, BLOCK), F32),
            pltpu.VMEM((blocks, head_count, BLOCK), F32),
            pltpu.VMEM((blocks, head_count, BLOCK), F32),
            pltpu.VMEM((blocks, states, BLOCK), BF16),
            pltpu.VMEM((blocks, BLOCK, BLOCK), F32),
            pltpu.VMEM((blocks, BLOCK, BLOCK), F32),
            pltpu.VMEM((chunks, wp, tok), F32),
            pltpu.VMEM((chunks, wp, tok), BF16),
            pltpu.VMEM((chunks, rows, wp), F32),
            pltpu.VMEM((chunks, blocks - 1, rows, wp), F32),
            pltpu.VMEM((chunks, PLANE, rows, wq), F32),
            pltpu.VMEM((chunks, states, wq), F32),
            pltpu.VMEM((chunks, states, wq), F32),
            pltpu.VMEM((chunks, PLANE, states, wq), F32),
            pltpu.VMEM((chunks, PLANE, states, wq), F32),
            dma((2, chunks)),
            dma((5,)),
            dma((chunks,)),
            dma((1,)),
            dma((1,)),
            dma((G, 2)),
            dma((G, 2)),
            dma((chunks, PLANE)),
            dma((chunks, PLANE)),
            dma((chunks,)),
            dma((chunks,)),
            dma((chunks, PLANE)),
            dma((chunks, PLANE)),
        ],
        compiler_params=pltpu.CompilerParams(
            collective_id=0, has_side_effects=True, vmem_limit_bytes=VLIM),
        name="prefill",
    )(*[pltpu.with_memory_space_constraint(part_, pltpu.HBM) for part_ in (
        prompt_sizes, skip_gain, log_rates.reshape(1, head_count), packing,
        inputs, projections, step_sizes)])


def solution(mesh):
    in_specs = (
        P(None, ("groups", "ctx")),
        P(None, ("groups", "ctx")),
        P(None, ("groups", "ctx")),
        P(),
        P(),
        P(("groups", "ctx"), None),
        P("groups"),
    )
    out_specs = P(None, ("groups", "ctx"))
    return jax.shard_map(
        functools.partial(per_device, mesh.shape["ctx"]),
        mesh=mesh, in_specs=in_specs, out_specs=out_specs, check_vma=False,
    )
```

```python
import functools
import jax
import jax.numpy as jnp
from jax import lax
from jax.experimental import pallas as pl
from jax.experimental.pallas import tpu as pltpu
from jax.sharding import PartitionSpec as P

G = 4
BLOCK = 128
LANES = 128
PLANE = 4
LAGS = (1,2,4,5)
LAST_DONE = (7,6,4,3)
NEXT_DONE = (7,5,3,2)
VLIM = 36 * 1024 * 1024
F32 = jnp.float32
BF16 = jnp.bfloat16
MESH = pl.DeviceIdType.MESH


def dot_nt(a, b):
    return lax.dot_general(a, b, (((1,), (1,)), ((), ())), preferred_element_type=F32)


def starts_of(sizes_ref):
    out = []
    at = jnp.int32(0)
    for s in range(sizes_ref.shape[0]):
        out.append(at)
        at = at + sizes_ref[s]
    return out


def segment_of(position, starts):
    seg = jnp.zeros(position.shape, jnp.int32)
    for at in starts:
        seg = seg + (position >= at).astype(jnp.int32)
    return seg


def decay_of(dt, rate):
    t = dt.shape[0]
    tri = jnp.where(
        lax.broadcasted_iota(jnp.int32, (t, t), 0) >= lax.broadcasted_iota(jnp.int32, (t, t), 1),
        1.0, 0.0).astype(F32)
    return jnp.dot(tri, dt * rate, preferred_element_type=F32, precision=lax.Precision.HIGHEST)


def spread(value, heads, width):
    rows = value.shape[0]
    per = LANES // width
    lane = lax.broadcasted_iota(jnp.int32, (rows, LANES), 1)
    out = []
    for q in range(heads // per):
        acc = jnp.broadcast_to(value[:, q * per:q * per + 1], (rows, LANES))
        for k in range(1, per):
            other = jnp.broadcast_to(value[:, q * per + k:q * per + k + 1], (rows, LANES))
            acc = jnp.where(lane >= k * width, other, acc)
        out.append(acc)
    return jnp.concatenate(out, axis=1)


def fused_kernel(
    n, heads, width, states,
    sizes_hbm, skip_hbm, rate_hbm, pack_hbm, x_hbm, bc_hbm, dt_hbm, o_ref,
    sizes_ref, skip_ref, rate_ref, pack_ref, dt_ref,
    xv, bv, pick, ys, yr, ds, dr,
    cum_g, into_g, keep_g, cum_t, dt_t, opens, maps_t, gram, allow, acc,
    t_own, t0, t_in, enter, leave, out_e, carry, k_own, k_in, gains, p_own, p_in,
    in_sem, few_sem, ds_sem, dr_sem, ys_sem, yr_sem,
    ts_sem, tr_sem, es_sem, er_sem, cs_sem, cr_sem, ks_sem, kr_sem, ps_sem, pr_sem,
):
    me = lax.axis_index("ctx")
    tok = dt_ref.shape[1]
    slot = tok // n
    part = heads // 2
    wp = part * width
    wx = heads * width
    wm = 2 * states
    wq = wp // PLANE
    chunks = 2 * G
    blocks = tok // BLOCK
    half = n // 2
    q = lax.rem(me, PLANE)
    z = me // PLANE
    nz = n // PLANE
    base = me * tok

    def by_plane(values):
        return jnp.where(z == 0, values[0], jnp.where(
            z < nz // 2, values[1], jnp.where(z < nz - 1, values[2], values[3])))

    lag = by_plane(LAGS)

    def loop(count, body, low=0):
        def step(i, _):
            body(i)
            return 0
        lax.fori_loop(low, count, step, 0)

    def load_x(c):
        r = pl.ds(pl.multiple_of(c * wp, LANES), wp)
        return pltpu.make_async_copy(x_hbm.at[r], xv.at[c], in_sem.at[0, c])

    def load_m(g):
        r = pl.ds(pl.multiple_of(g * wm, LANES), wm)
        return pltpu.make_async_copy(bc_hbm.at[r], bv.at[g], in_sem.at[1, g])

    few = [
        pltpu.make_async_copy(src, dst, few_sem.at[i])
        for i, (src, dst) in enumerate((
            (pack_hbm, pack_ref), (dt_hbm, dt_ref), (sizes_hbm, sizes_ref),
            (skip_hbm, skip_ref), (rate_hbm, rate_ref)))
    ]
    few[0].start()
    few[1].start()
    load_m(0).start()
    load_x(0).start()
    load_x(1).start()

    barrier = pltpu.get_barrier_semaphore()
    loop(n, lambda off: pl.semaphore_signal(
        barrier, inc=1, device_id={"ctx": lax.rem(me + off, n)}, device_id_type=MESH), low=1)

    for copy in few[2:]:
        copy.start()
    loop(G, lambda g: load_m(g).start(), low=1)
    loop(chunks, lambda c: load_x(c).start(), low=2)
    few[0].wait()

    rows = lax.broadcasted_iota(jnp.int32, (tok, tok), 0)
    pick[...] = jnp.where(rows == pack_ref[...], 1.0, 0.0).astype(F32).T.astype(BF16)
    head_count = dt_ref.shape[0]
    few[1].wait()
    dt_all = dot_nt(pick[...], dt_ref[...]).astype(BF16)
    dt_all = jnp.concatenate([dt_all, jnp.zeros((tok, LANES - head_count), BF16)], axis=1)
    ds[...] = dt_all.reshape(n, slot, LANES)

    def lanes_of(k):
        return slice(0, wm + wp) if k == 0 else slice(wm + wp, wm + wx)

    def prep(g, k):
        if k == 0:
            load_m(g).wait()
            ys[g, :, :, :wm] = dot_nt(pick[...], bv[g]).astype(BF16).reshape(n, slot, wm)
        load_x(2 * g + k).wait()
        y = dot_nt(pick[...], xv[2 * g + k]).astype(BF16)
        ys[g, :, :, wm + k * wp:wm + (k + 1) * wp] = y.reshape(n, slot, wp)

    def send_y(g, k, off):
        to = lax.rem(me + off, n)
        s = lanes_of(k)
        return pltpu.make_async_remote_copy(
            ys.at[g, to, :, s], yr.at[g, me, :, s], ys_sem.at[g, k], yr_sem.at[g, k],
            device_id={"ctx": to}, device_id_type=MESH)

    def send_d(off):
        to = lax.rem(me + off, n)
        return pltpu.make_async_remote_copy(
            ds.at[to], dr.at[me], ds_sem.at[0], dr_sem.at[0],
            device_id={"ctx": to}, device_id_type=MESH)

    def spread_out(send):
        def pair(i):
            send(half - i).start()

            @pl.when(i > 0)
            def _():
                send(half + i).start()

        loop(half, pair)

    def issue(g, k):
        s = lanes_of(k)
        spread_out(lambda off: send_y(g, k, off))
        pltpu.make_async_copy(ys.at[g, me, :, s], yr.at[g, me, :, s], yr_sem.at[g, k]).start()

    def arrived(g, k):
        s = lanes_of(k)
        pltpu.make_async_copy(ys.at[g, :, :, s], yr.at[g, :, :, s], yr_sem.at[g, k]).wait()

    def departed(g, k):
        s = lanes_of(k)
        most = slice(0, n - 1)
        pltpu.make_async_copy(ys.at[g, most, :, s], yr.at[g, most, :, s], ys_sem.at[g, k]).wait()

    prep(0, 0)
    pl.semaphore_wait(barrier, n - 1)
    spread_out(send_d)
    pltpu.make_async_copy(ds.at[me], dr.at[me], dr_sem.at[0]).start()
    issue(0, 0)
    prep(0, 1)
    issue(0, 1)

    def prep_rest(g):
        prep(g, 0)
        prep(g, 1)

    loop(G, prep_rest, low=1)

    for copy in few[2:]:
        copy.wait()
    starts = starts_of(sizes_ref)
    rate = jnp.concatenate(
        [rate_ref[...], jnp.zeros((1, LANES - head_count), F32)], axis=1)
    rate = jnp.broadcast_to(-jnp.exp(rate), (8, LANES))[0:1]

    pltpu.make_async_copy(ds, dr, dr_sem.at[0]).wait()

    def rows_of(b):
        return slice(b * BLOCK // slot, (b + 1) * BLOCK // slot)

    for b in range(blocks):
        head = base + b * BLOCK
        last = head + BLOCK - 1
        dt = dr[rows_of(b)].reshape(BLOCK, LANES).astype(F32)
        cum = decay_of(dt, rate)
        end = cum[BLOCK - 1:BLOCK, :]
        pos = head + lax.broadcasted_iota(jnp.int32, (BLOCK, LANES), 0)
        last_seg = jnp.int32(0)
        cut = jnp.int32(0)
        for at in starts:
            last_seg = last_seg + (last >= at).astype(jnp.int32)
            cut = cut + ((at >= head) & (at <= last)).astype(jnp.int32)
        same = segment_of(pos, starts) == last_seg
        into = jnp.where(same, jnp.exp(end - cum), 0.0) * dt
        keep = jnp.broadcast_to(jnp.where(cut == 0, jnp.exp(end), 0.0), (8, LANES))
        for g in range(G):
            shift = (LANES - g * heads) % LANES
            cum_g[g, b] = pltpu.roll(cum, shift, 1)
            into_g[g, b] = pltpu.roll(into, shift, 1)
            keep_g[g, b] = pltpu.roll(keep, shift, 1)
        across = cum.T[:head_count]
        cum_t[b] = across
        dt_t[b] = dt.T[:head_count]
        row_pos = head + lax.broadcasted_iota(jnp.int32, (1, BLOCK), 1)
        row_cut = jnp.zeros((1, BLOCK), jnp.int32)
        for at in starts:
            row_cut = row_cut + ((row_pos >= at) & (at >= head)).astype(jnp.int32)
        opens[b] = jnp.where(row_cut == 0, jnp.exp(across), 0.0)
        pos_i = head + lax.broadcasted_iota(jnp.int32, (BLOCK, BLOCK), 0)
        pos_j = head + lax.broadcasted_iota(jnp.int32, (BLOCK, BLOCK), 1)
        fits = (pos_i >= pos_j) & (segment_of(pos_i, starts) == segment_of(pos_j, starts))
        allow[b] = jnp.where(fits, 0.0, -jnp.inf)

    for g in range(G):
        keep = keep_g[g, 0]
        for b in range(1, blocks):
            keep = keep * keep_g[g, b]
        k_own[g] = keep

    def send_keep(hop):
        return pltpu.make_async_remote_copy(
            k_own, k_in.at[q], ks_sem.at[hop], kr_sem.at[hop],
            device_id={"ctx": z * PLANE + lax.rem(q + hop, PLANE)}, device_id_type=MESH)

    own_keep = pltpu.make_async_copy(k_own, k_in.at[q], kr_sem.at[0])
    for hop in range(1, PLANE):
        send_keep(hop).start()
    own_keep.start()

    def y_of(g, b, lo, hi):
        return yr[g, rows_of(b), :, lo:hi].reshape(BLOCK, hi - lo)

    def x_of(g, k, b):
        return y_of(g, b, wm + k * wp, wm + (k + 1) * wp)

    def quarter(k):
        return slice(k * wq, (k + 1) * wq)

    def send_total(c, hop):
        to = lax.rem(q + hop, PLANE)
        s = pl.ds(pl.multiple_of(to * wq, LANES), wq)
        return pltpu.make_async_remote_copy(
            t_own.at[c, :, s], t_in.at[c, q], ts_sem.at[c, hop], tr_sem.at[c, hop],
            device_id={"ctx": z * PLANE + to}, device_id_type=MESH)

    def own_total(c):
        s = pl.ds(pl.multiple_of(q * wq, LANES), wq)
        return pltpu.make_async_copy(t_own.at[c, :, s], t_in.at[c, q], tr_sem.at[c, 0])

    def send_leave(c):
        return pltpu.make_async_remote_copy(
            leave.at[c], enter.at[c], es_sem.at[c], er_sem.at[c],
            device_id={"ctx": me + PLANE}, device_id_type=MESH)

    def take_enter(c):
        return pltpu.make_async_remote_copy(
            leave.at[c], enter.at[c], es_sem.at[c], er_sem.at[c],
            device_id={"ctx": me - PLANE}, device_id_type=MESH)

    def send_entering(c, hop):
        to = lax.rem(q + hop, PLANE)
        return pltpu.make_async_remote_copy(
            out_e.at[c, to], carry.at[c, q], cs_sem.at[c, hop], cr_sem.at[c, hop],
            device_id={"ctx": z * PLANE + to}, device_id_type=MESH)

    def own_entering(c):
        return pltpu.make_async_copy(out_e.at[c, q], carry.at[c, q], cr_sem.at[c, 0])

    def states_stage(g, k):
        c = 2 * g + k
        total = None
        for b in range(blocks):
            if k == 0:
                in_map = y_of(g, b, 0, states)
                out_map = y_of(g, b, states, wm)
                maps_t[b] = in_map.astype(F32).T.astype(BF16)
                gram[b] = dot_nt(out_map, in_map)
            cols = slice(k * part, (k + 1) * part)
            into = spread(into_g[g, b][:, cols], part, width)
            weighted = (x_of(g, k, b).astype(F32) * into).astype(BF16)
            block_total = jnp.dot(maps_t[b], weighted, preferred_element_type=F32)
            keep = spread(keep_g[g, b][:, cols], part, width)
            if total is None:
                total = block_total
            else:
                total = keep[0:1] * total + block_total
            if b < blocks - 1:
                t0[c, b, :states, :] = block_total
                t0[c, b, states:, :] = keep
        t_own[c] = total
        for hop in range(1, PLANE):
            send_total(c, hop).start()
        own_total(c).start()

    def inner_stage(g, k):
        c = 2 * g + k
        first = pl.multiple_of(c * part, part)
        for b in range(blocks):
            lo = b * BLOCK
            cum = cum_g[g, b]
            across = cum_t[b, pl.ds(first, part), :]
            dt = dt_t[b, pl.ds(first, part), :]
            x_fm = x_of(g, k, b).T
            for h in range(part):
                col = k * part + h
                gap = jnp.broadcast_to(cum[:, col:col + 1], (BLOCK, BLOCK)) - across[h:h + 1]
                mask = jnp.exp(gap + allow[b])
                mixing = (gram[b] * (mask * dt[h:h + 1])).astype(BF16)
                r = slice(h * width, (h + 1) * width)
                xh = x_fm[r]
                acc[c, r, lo:lo + BLOCK] = (
                    dot_nt(xh, mixing) + skip_ref[c * part + h] * xh.astype(F32))

    end = chunks - 1

    def totals_in(c):
        for hop in range(1, PLANE):
            send_total(c, hop).wait_recv()
        own_total(c).wait()

    def hand_out(c, state):
        for k in range(PLANE):
            out_e[c, k] = state
            if k < PLANE - 1:
                state = gains[c, k, 0:1] * state + t_in[c, k]
        for hop in range(1, PLANE):
            send_entering(c, hop).start()
        own_entering(c).start()

    def chain_stage(c):
        totals_in(c)

        @pl.when(z > 0)
        def _():
            take_enter(c).wait_recv()

        @pl.when(z == 0)
        def _():
            enter[c] = jnp.zeros((states, wq), F32)

        @pl.when(z < nz - 1)
        def _():
            state = enter[c]
            for k in range(PLANE):
                state = gains[c, k, 0:1] * state + t_in[c, k]
            leave[c] = state
            send_leave(c).start()

        hand_out(c, enter[c])

    def send_plane(to):
        return pltpu.make_async_remote_copy(
            p_own, p_in.at[z], ps_sem.at[to], pr_sem.at[z],
            device_id={"ctx": to * PLANE + q}, device_id_type=MESH)

    def take_plane(at):
        return pltpu.make_async_remote_copy(
            p_own, p_in.at[at], ps_sem.at[at], pr_sem.at[at],
            device_id={"ctx": at * PLANE + q}, device_id_type=MESH)

    def announce():
        totals_in(end)

        @pl.when(z < nz - 1)
        def _():
            total, gain = t_in[end, 0], gains[end, 0]
            for k in range(1, PLANE):
                total = gains[end, k, 0:1] * total + t_in[end, k]
                gain = gain * gains[end, k]
            p_own[:states] = total
            p_own[states:] = gain
            loop(nz - 1 - z, lambda i: send_plane(nz - 1 - i).start())

    def close_chain():
        enter[end] = jnp.zeros((states, wq), F32)

        def add(at):
            take_plane(at).wait_recv()
            enter[end] = p_in[at, states:states + 1] * enter[end] + p_in[at, :states]

        loop(z, add)
        hand_out(end, enter[end])

    def output_stage(c):
        for hop in range(1, PLANE):
            send_entering(c, hop).wait_recv()
        own_entering(c).wait()
        g = c // 2
        first = pl.multiple_of(c * part, part)
        state = jnp.concatenate([carry[c, k] for k in range(PLANE)], axis=1)
        for b in range(blocks):
            lo = b * BLOCK
            out_map = y_of(g, b, states, wm)
            carried = dot_nt(state.astype(BF16).T, out_map)
            opened = opens[b, pl.ds(first, part), :]
            for h in range(part):
                r = slice(h * width, (h + 1) * width)
                o_ref[pl.ds(pl.multiple_of(c * wp + h * width, width), width), lo:lo + BLOCK] = (
                    acc[c, r, lo:lo + BLOCK] + carried[r] * opened[h:h + 1]).astype(BF16)
            if b < blocks - 1:
                state = t0[c, b, states:states + 1, :] * state + t0[c, b, :states, :]

    lane = lax.broadcasted_iota(jnp.int32, (8, wq), 1)

    def widen(c):
        first = lax.rem(c, 2) * part + q * (wq // width)
        for k in range(PLANE):
            keep = pltpu.roll(k_in[k, c // 2], lax.rem(LANES - first, LANES), 1)
            gain = jnp.broadcast_to(keep[:, 0:1], (8, wq))
            for h in range(1, wq // width):
                gain = jnp.where(lane >= h * width, jnp.broadcast_to(keep[:, h:h + 1], (8, wq)), gain)
            gains[c, k] = gain

    def done_by(step):
        due = jnp.maximum(step + 1 - lag, 0)
        due = jnp.where(step == end - 1, by_plane(NEXT_DONE), due)
        return jnp.where(step == end, by_plane(LAST_DONE), due)

    def follow(step):
        loop(done_by(step), chain_stage, low=done_by(step - 1))
        loop(done_by(step) - 1, output_stage, low=jnp.maximum(done_by(step - 1) - 1, 0))

    def turn(g):
        for k in range(2):
            arrived(g, k)

            @pl.when(g < G - 1)
            def _():
                issue(g + 1, k)

            states_stage(g, k)
            inner_stage(g, k)
            if k == 0:
                @pl.when(g == 0)
                def _():
                    own_keep.wait()
                    for hop in range(1, PLANE):
                        send_keep(hop).wait_recv()
                    loop(chunks, widen)

            follow(2 * g + k)

    loop(G, turn)
    done = by_plane(LAST_DONE)
    early = jnp.maximum(done - 1, jnp.where(z >= nz // 2, end - 3, 0))
    near = jnp.where(z < nz // 2, end, end - 1)
    loop(near, chain_stage, low=done)
    loop(early, output_stage, low=done - 1)
    announce()
    loop(end, chain_stage, low=near)
    close_chain()
    loop(chunks, output_stage, low=early)

    most = slice(0, n - 1)
    pltpu.make_async_copy(ds.at[most], dr.at[most], ds_sem.at[0]).wait()
    for hop in range(1, PLANE):
        send_keep(hop).wait_send()

    def close(g):
        for k in range(2):
            departed(g, k)
            c = 2 * g + k
            for hop in range(1, PLANE):
                send_total(c, hop).wait_send()
                send_entering(c, hop).wait_send()

            @pl.when((z < nz - 1) & (c < end))
            def _():
                send_leave(c).wait_send()


    loop(G, close)
    loop(nz, lambda at: send_plane(at).wait_send(), low=z + 1)


def per_device(n, inputs, projections, step_sizes, log_rates, skip_gain, packing, prompt_sizes):
    tok = inputs.shape[1]
    head_count = log_rates.shape[0]
    heads = head_count // G
    states = projections.shape[0] // (2 * G)
    width = inputs.shape[0] // head_count
    part = heads // 2
    wp = part * width
    wx = heads * width
    wm = 2 * states
    wq = wp // PLANE
    slot = tok // n
    blocks = tok // BLOCK
    rows = states + 8
    nz = n // PLANE
    chunks = 2 * G
    hbm = pl.BlockSpec(memory_space=pltpu.HBM)
    dma = pltpu.SemaphoreType.DMA
    return pl.pallas_call(
        functools.partial(fused_kernel, n, heads, width, states),
        in_specs=[hbm] * 7,
        out_specs=pl.BlockSpec(memory_space=pltpu.VMEM),
        out_shape=jax.ShapeDtypeStruct((G * wx, tok), BF16),
        scratch_shapes=[
            pltpu.SMEM(prompt_sizes.shape, jnp.int32),
            pltpu.SMEM(skip_gain.shape, F32),
            pltpu.VMEM((1, head_count), F32),
            pltpu.VMEM((1, tok), jnp.int32),
            pltpu.VMEM((head_count, tok), BF16),
            pltpu.VMEM((chunks, wp, tok), BF16),
            pltpu.VMEM((G, wm, tok), BF16),
            pltpu.VMEM((tok, tok), BF16),
            pltpu.VMEM((G, n, slot, wm + wx), BF16),
            pltpu.VMEM((G, n, slot, wm + wx), BF16),
            pltpu.VMEM((n, slot, LANES), BF16),
            pltpu.VMEM((n, slot, LANES), BF16),
            pltpu.VMEM((G, blocks, BLOCK, LANES), F32),
            pltpu.VMEM((G, blocks, BLOCK, LANES), F32),
            pltpu.VMEM((G, blocks, 8, LANES), F32),
            pltpu.VMEM((blocks, head_count, BLOCK), F32),
            pltpu.VMEM((blocks, head_count, BLOCK), F32),
            pltpu.VMEM((blocks, head_count, BLOCK), F32),
            pltpu.VMEM((blocks, states, BLOCK), BF16),
            pltpu.VMEM((blocks, BLOCK, BLOCK), F32),
            pltpu.VMEM((blocks, BLOCK, BLOCK), F32),
            pltpu.VMEM((chunks, wp, tok), F32),
            pltpu.VMEM((chunks, states, wp), F32),
            pltpu.VMEM((chunks, blocks - 1, rows, wp), F32),
            pltpu.VMEM((chunks, PLANE, states, wq), F32),
            pltpu.VMEM((chunks, states, wq), F32),
            pltpu.VMEM((chunks, states, wq), F32),
            pltpu.VMEM((chunks, PLANE, states, wq), F32),
            pltpu.VMEM((chunks, PLANE, states, wq), F32),
            pltpu.VMEM((G, 8, LANES), F32),
            pltpu.VMEM((PLANE, G, 8, LANES), F32),
            pltpu.VMEM((chunks, PLANE, 8, wq), F32),
            pltpu.VMEM((states + 8, wq), F32),
            pltpu.VMEM((nz, states + 8, wq), F32),
            dma((2, chunks)),
            dma((5,)),
            dma((1,)),
            dma((1,)),
            dma((G, 2)),
            dma((G, 2)),
            dma((chunks, PLANE)),
            dma((chunks, PLANE)),
            dma((chunks,)),
            dma((chunks,)),
            dma((chunks, PLANE)),
            dma((chunks, PLANE)),
            dma((PLANE,)),
            dma((PLANE,)),
            dma((nz,)),
            dma((nz,)),
        ],
        compiler_params=pltpu.CompilerParams(
            collective_id=0, has_side_effects=True, vmem_limit_bytes=VLIM),
        name="prefill",
    )(*[pltpu.with_memory_space_constraint(part_, pltpu.HBM) for part_ in (
        prompt_sizes, skip_gain, log_rates.reshape(1, head_count), packing,
        inputs, projections, step_sizes)])


def solution(mesh):
    in_specs = (
        P(None, ("groups", "ctx")),
        P(None, ("groups", "ctx")),
        P(None, ("groups", "ctx")),
        P(),
        P(),
        P(("groups", "ctx"), None),
        P("groups"),
    )
    out_specs = P(None, ("groups", "ctx"))
    return jax.shard_map(
        functools.partial(per_device, mesh.shape["ctx"]),
        mesh=mesh, in_specs=in_specs, out_specs=out_specs, check_vma=False,
    )
```

```python
import functools
import jax
import jax.numpy as jnp
from jax import lax
from jax.experimental import pallas as pl
from jax.experimental.pallas import tpu as pltpu
from jax.sharding import PartitionSpec as P

G = 4
BLOCK = 128
LANES = 128
PLANE = 4
LAGS = (1,2,4,5)
LAST_DONE = (7,6,4,3)
NEXT_DONE = (7,5,3,2)
OUT_LAGS = (1,1,2,2)
VLIM = 36 * 1024 * 1024
F32 = jnp.float32
BF16 = jnp.bfloat16
MESH = pl.DeviceIdType.MESH


def dot_nt(a, b):
    return lax.dot_general(a, b, (((1,), (1,)), ((), ())), preferred_element_type=F32)


def starts_of(sizes_ref):
    out = []
    at = jnp.int32(0)
    for s in range(sizes_ref.shape[0]):
        out.append(at)
        at = at + sizes_ref[s]
    return out


def segment_of(position, starts):
    seg = jnp.zeros(position.shape, jnp.int32)
    for at in starts:
        seg = seg + (position >= at).astype(jnp.int32)
    return seg


def decay_of(dt, rate):
    t = dt.shape[0]
    tri = jnp.where(
        lax.broadcasted_iota(jnp.int32, (t, t), 0) >= lax.broadcasted_iota(jnp.int32, (t, t), 1),
        1.0, 0.0).astype(F32)
    return jnp.dot(tri, dt * rate, preferred_element_type=F32, precision=lax.Precision.HIGHEST)


def spread(value, heads, width):
    rows = value.shape[0]
    per = LANES // width
    lane = lax.broadcasted_iota(jnp.int32, (rows, LANES), 1)
    out = []
    for q in range(heads // per):
        acc = jnp.broadcast_to(value[:, q * per:q * per + 1], (rows, LANES))
        for k in range(1, per):
            other = jnp.broadcast_to(value[:, q * per + k:q * per + k + 1], (rows, LANES))
            acc = jnp.where(lane >= k * width, other, acc)
        out.append(acc)
    return jnp.concatenate(out, axis=1)


def fused_kernel(
    n, heads, width, states,
    sizes_hbm, skip_hbm, rate_hbm, pack_hbm, x_hbm, bc_hbm, dt_hbm, o_ref,
    sizes_ref, skip_ref, rate_ref, pack_ref, dt_ref,
    xv, bv, pick, ys, yr, ds, dr,
    cum_g, into_g, keep_g, cum_t, dt_t, opens, maps_t, gram, allow, acc,
    t_own, t0, t_in, enter, leave, out_e, carry, k_own, k_in, gains, p_own, p_in,
    in_sem, few_sem, ds_sem, dr_sem, ys_sem, yr_sem,
    ts_sem, tr_sem, es_sem, er_sem, cs_sem, cr_sem, ks_sem, kr_sem, ps_sem, pr_sem,
):
    me = lax.axis_index("ctx")
    tok = dt_ref.shape[1]
    slot = tok // n
    part = heads // 2
    wp = part * width
    wx = heads * width
    wm = 2 * states
    wq = wp // PLANE
    chunks = 2 * G
    blocks = tok // BLOCK
    half = n // 2
    q = lax.rem(me, PLANE)
    z = me // PLANE
    nz = n // PLANE
    base = me * tok

    def by_plane(values):
        return jnp.where(z == 0, values[0], jnp.where(
            z < nz // 2, values[1], jnp.where(z < nz - 1, values[2], values[3])))

    lag = by_plane(LAGS)

    def loop(count, body, low=0):
        def step(i, _):
            body(i)
            return 0
        lax.fori_loop(low, count, step, 0)

    def load_x(c):
        r = pl.ds(pl.multiple_of(c * wp, LANES), wp)
        return pltpu.make_async_copy(x_hbm.at[r], xv.at[c], in_sem.at[0, c])

    def load_m(g):
        r = pl.ds(pl.multiple_of(g * wm, LANES), wm)
        return pltpu.make_async_copy(bc_hbm.at[r], bv.at[g], in_sem.at[1, g])

    few = [
        pltpu.make_async_copy(src, dst, few_sem.at[i])
        for i, (src, dst) in enumerate((
            (pack_hbm, pack_ref), (dt_hbm, dt_ref), (sizes_hbm, sizes_ref),
            (skip_hbm, skip_ref), (rate_hbm, rate_ref)))
    ]
    few[0].start()
    few[1].start()
    load_m(0).start()
    load_x(0).start()
    load_x(1).start()

    barrier = pltpu.get_barrier_semaphore()
    loop(n, lambda off: pl.semaphore_signal(
        barrier, inc=1, device_id={"ctx": lax.rem(me + off, n)}, device_id_type=MESH), low=1)

    for copy in few[2:]:
        copy.start()
    loop(G, lambda g: load_m(g).start(), low=1)
    loop(chunks, lambda c: load_x(c).start(), low=2)
    few[0].wait()

    rows = lax.broadcasted_iota(jnp.int32, (tok, tok), 0)
    pick[...] = jnp.where(rows == pack_ref[...], 1.0, 0.0).astype(F32).T.astype(BF16)
    head_count = dt_ref.shape[0]
    few[1].wait()
    dt_all = dot_nt(pick[...], dt_ref[...]).astype(BF16)
    dt_all = jnp.concatenate([dt_all, jnp.zeros((tok, LANES - head_count), BF16)], axis=1)
    ds[...] = dt_all.reshape(n, slot, LANES)

    def lanes_of(k):
        return slice(0, wm + wp) if k == 0 else slice(wm + wp, wm + wx)

    def prep(g, k):
        if k == 0:
            load_m(g).wait()
            ys[g, :, :, :wm] = dot_nt(pick[...], bv[g]).astype(BF16).reshape(n, slot, wm)
        load_x(2 * g + k).wait()
        y = dot_nt(pick[...], xv[2 * g + k]).astype(BF16)
        ys[g, :, :, wm + k * wp:wm + (k + 1) * wp] = y.reshape(n, slot, wp)

    def send_y(g, k, off):
        to = lax.rem(me + off, n)
        s = lanes_of(k)
        return pltpu.make_async_remote_copy(
            ys.at[g, to, :, s], yr.at[g, me, :, s], ys_sem.at[g, k], yr_sem.at[g, k],
            device_id={"ctx": to}, device_id_type=MESH)

    def send_d(off):
        to = lax.rem(me + off, n)
        return pltpu.make_async_remote_copy(
            ds.at[to], dr.at[me], ds_sem.at[0], dr_sem.at[0],
            device_id={"ctx": to}, device_id_type=MESH)

    def spread_out(send):
        loop(n, lambda i: send(1 + lax.rem(2 * n - PLANE - 1 - i, n - 1)).start(), low=1)

    def issue(g, k):
        s = lanes_of(k)
        spread_out(lambda off: send_y(g, k, off))
        pltpu.make_async_copy(ys.at[g, me, :, s], yr.at[g, me, :, s], yr_sem.at[g, k]).start()

    def arrived(g, k):
        s = lanes_of(k)
        pltpu.make_async_copy(ys.at[g, :, :, s], yr.at[g, :, :, s], yr_sem.at[g, k]).wait()

    def departed(g, k):
        s = lanes_of(k)
        most = slice(0, n - 1)
        pltpu.make_async_copy(ys.at[g, most, :, s], yr.at[g, most, :, s], ys_sem.at[g, k]).wait()

    prep(0, 0)
    pl.semaphore_wait(barrier, n - 1)
    spread_out(send_d)
    pltpu.make_async_copy(ds.at[me], dr.at[me], dr_sem.at[0]).start()
    issue(0, 0)
    prep(0, 1)
    issue(0, 1)

    def prep_rest(g):
        prep(g, 0)
        prep(g, 1)

    loop(G, prep_rest, low=1)

    for copy in few[2:]:
        copy.wait()
    starts = starts_of(sizes_ref)
    rate = jnp.concatenate(
        [rate_ref[...], jnp.zeros((1, LANES - head_count), F32)], axis=1)
    rate = jnp.broadcast_to(-jnp.exp(rate), (8, LANES))[0:1]

    pltpu.make_async_copy(ds, dr, dr_sem.at[0]).wait()

    def rows_of(b):
        return slice(b * BLOCK // slot, (b + 1) * BLOCK // slot)

    for b in range(blocks):
        head = base + b * BLOCK
        last = head + BLOCK - 1
        dt = dr[rows_of(b)].reshape(BLOCK, LANES).astype(F32)
        cum = decay_of(dt, rate)
        end = cum[BLOCK - 1:BLOCK, :]
        pos = head + lax.broadcasted_iota(jnp.int32, (BLOCK, LANES), 0)
        last_seg = jnp.int32(0)
        cut = jnp.int32(0)
        for at in starts:
            last_seg = last_seg + (last >= at).astype(jnp.int32)
            cut = cut + ((at >= head) & (at <= last)).astype(jnp.int32)
        same = segment_of(pos, starts) == last_seg
        into = jnp.where(same, jnp.exp(end - cum), 0.0) * dt
        keep = jnp.broadcast_to(jnp.where(cut == 0, jnp.exp(end), 0.0), (8, LANES))
        for g in range(G):
            shift = (LANES - g * heads) % LANES
            cum_g[g, b] = pltpu.roll(cum, shift, 1)
            into_g[g, b] = pltpu.roll(into, shift, 1)
            keep_g[g, b] = pltpu.roll(keep, shift, 1)
        across = cum.T[:head_count]
        cum_t[b] = across
        dt_t[b] = dt.T[:head_count]
        row_pos = head + lax.broadcasted_iota(jnp.int32, (1, BLOCK), 1)
        row_cut = jnp.zeros((1, BLOCK), jnp.int32)
        for at in starts:
            row_cut = row_cut + ((row_pos >= at) & (at >= head)).astype(jnp.int32)
        opens[b] = jnp.where(row_cut == 0, jnp.exp(across), 0.0)
        pos_i = head + lax.broadcasted_iota(jnp.int32, (BLOCK, BLOCK), 0)
        pos_j = head + lax.broadcasted_iota(jnp.int32, (BLOCK, BLOCK), 1)
        fits = (pos_i >= pos_j) & (segment_of(pos_i, starts) == segment_of(pos_j, starts))
        allow[b] = jnp.where(fits, 0.0, -jnp.inf)

    for g in range(G):
        keep = keep_g[g, 0]
        for b in range(1, blocks):
            keep = keep * keep_g[g, b]
        k_own[g] = keep

    def send_keep(hop):
        return pltpu.make_async_remote_copy(
            k_own, k_in.at[q], ks_sem.at[hop], kr_sem.at[hop],
            device_id={"ctx": z * PLANE + lax.rem(q + hop, PLANE)}, device_id_type=MESH)

    own_keep = pltpu.make_async_copy(k_own, k_in.at[q], kr_sem.at[0])
    for hop in range(1, PLANE):
        send_keep(hop).start()
    own_keep.start()

    def y_of(g, b, lo, hi):
        return yr[g, rows_of(b), :, lo:hi].reshape(BLOCK, hi - lo)

    def x_of(g, k, b):
        return y_of(g, b, wm + k * wp, wm + (k + 1) * wp)

    def quarter(k):
        return slice(k * wq, (k + 1) * wq)

    def send_total(c, hop):
        to = lax.rem(q + hop, PLANE)
        s = pl.ds(pl.multiple_of(to * wq, LANES), wq)
        return pltpu.make_async_remote_copy(
            t_own.at[c, :, s], t_in.at[c, q], ts_sem.at[c, hop], tr_sem.at[c, hop],
            device_id={"ctx": z * PLANE + to}, device_id_type=MESH)

    def own_total(c):
        s = pl.ds(pl.multiple_of(q * wq, LANES), wq)
        return pltpu.make_async_copy(t_own.at[c, :, s], t_in.at[c, q], tr_sem.at[c, 0])

    def send_leave(c):
        return pltpu.make_async_remote_copy(
            leave.at[c], enter.at[c], es_sem.at[c], er_sem.at[c],
            device_id={"ctx": me + PLANE}, device_id_type=MESH)

    def take_enter(c):
        return pltpu.make_async_remote_copy(
            leave.at[c], enter.at[c], es_sem.at[c], er_sem.at[c],
            device_id={"ctx": me - PLANE}, device_id_type=MESH)

    def send_entering(c, hop):
        to = lax.rem(q + hop, PLANE)
        return pltpu.make_async_remote_copy(
            out_e.at[c, to], carry.at[c, q], cs_sem.at[c, hop], cr_sem.at[c, hop],
            device_id={"ctx": z * PLANE + to}, device_id_type=MESH)

    def own_entering(c):
        return pltpu.make_async_copy(out_e.at[c, q], carry.at[c, q], cr_sem.at[c, 0])

    def states_stage(g, k):
        c = 2 * g + k
        total = None
        for b in range(blocks):
            if k == 0:
                in_map = y_of(g, b, 0, states)
                out_map = y_of(g, b, states, wm)
                maps_t[b] = in_map.astype(F32).T.astype(BF16)
                gram[b] = dot_nt(out_map, in_map)
            cols = slice(k * part, (k + 1) * part)
            into = spread(into_g[g, b][:, cols], part, width)
            weighted = (x_of(g, k, b).astype(F32) * into).astype(BF16)
            block_total = jnp.dot(maps_t[b], weighted, preferred_element_type=F32)
            keep = spread(keep_g[g, b][:, cols], part, width)
            if total is None:
                total = block_total
            else:
                total = keep[0:1] * total + block_total
            if b < blocks - 1:
                t0[c, b, :states, :] = block_total
                t0[c, b, states:, :] = keep
        t_own[c] = total
        for hop in range(1, PLANE):
            send_total(c, hop).start()
        own_total(c).start()

    def inner_stage(g, k):
        c = 2 * g + k
        first = pl.multiple_of(c * part, part)
        for b in range(blocks):
            lo = b * BLOCK
            cum = cum_g[g, b]
            across = cum_t[b, pl.ds(first, part), :]
            dt = dt_t[b, pl.ds(first, part), :]
            x_fm = x_of(g, k, b).T
            for h in range(part):
                col = k * part + h
                gap = jnp.broadcast_to(cum[:, col:col + 1], (BLOCK, BLOCK)) - across[h:h + 1]
                mask = jnp.exp(gap + allow[b])
                mixing = (gram[b] * (mask * dt[h:h + 1])).astype(BF16)
                r = slice(h * width, (h + 1) * width)
                xh = x_fm[r]
                acc[c, r, lo:lo + BLOCK] = (
                    dot_nt(xh, mixing) + skip_ref[c * part + h] * xh.astype(F32))

    end = chunks - 1

    def totals_in(c):
        for hop in range(1, PLANE):
            send_total(c, hop).wait_recv()
        own_total(c).wait()

    def hand_out(c, state):
        for k in range(PLANE):
            out_e[c, k] = state
            if k < PLANE - 1:
                state = gains[c, k, 0:1] * state + t_in[c, k]
        for hop in range(1, PLANE):
            send_entering(c, hop).start()
        own_entering(c).start()

    def chain_stage(c):
        totals_in(c)

        @pl.when(z > 0)
        def _():
            take_enter(c).wait_recv()

        @pl.when(z == 0)
        def _():
            enter[c] = jnp.zeros((states, wq), F32)

        @pl.when(z < nz - 1)
        def _():
            state = enter[c]
            for k in range(PLANE):
                state = gains[c, k, 0:1] * state + t_in[c, k]
            leave[c] = state
            send_leave(c).start()

        hand_out(c, enter[c])

    def send_plane(to):
        return pltpu.make_async_remote_copy(
            p_own, p_in.at[z], ps_sem.at[to], pr_sem.at[z],
            device_id={"ctx": to * PLANE + q}, device_id_type=MESH)

    def take_plane(at):
        return pltpu.make_async_remote_copy(
            p_own, p_in.at[at], ps_sem.at[at], pr_sem.at[at],
            device_id={"ctx": at * PLANE + q}, device_id_type=MESH)

    def announce():
        totals_in(end)

        @pl.when(z < nz - 1)
        def _():
            total, gain = t_in[end, 0], gains[end, 0]
            for k in range(1, PLANE):
                total = gains[end, k, 0:1] * total + t_in[end, k]
                gain = gain * gains[end, k]
            p_own[:states] = total
            p_own[states:] = gain
            loop(nz - 1 - z, lambda i: send_plane(nz - 1 - i).start())

    def close_chain():
        enter[end] = jnp.zeros((states, wq), F32)

        def add(at):
            take_plane(at).wait_recv()
            enter[end] = p_in[at, states:states + 1] * enter[end] + p_in[at, :states]

        loop(z, add)
        hand_out(end, enter[end])

    def output_stage(c):
        for hop in range(1, PLANE):
            send_entering(c, hop).wait_recv()
        own_entering(c).wait()
        g = c // 2
        first = pl.multiple_of(c * part, part)
        state = jnp.concatenate([carry[c, k] for k in range(PLANE)], axis=1)
        for b in range(blocks):
            lo = b * BLOCK
            out_map = y_of(g, b, states, wm)
            carried = dot_nt(state.astype(BF16).T, out_map)
            opened = opens[b, pl.ds(first, part), :]
            for h in range(part):
                r = slice(h * width, (h + 1) * width)
                o_ref[pl.ds(pl.multiple_of(c * wp + h * width, width), width), lo:lo + BLOCK] = (
                    acc[c, r, lo:lo + BLOCK] + carried[r] * opened[h:h + 1]).astype(BF16)
            if b < blocks - 1:
                state = t0[c, b, states:states + 1, :] * state + t0[c, b, :states, :]

    lane = lax.broadcasted_iota(jnp.int32, (8, wq), 1)

    def widen(c):
        first = lax.rem(c, 2) * part + q * (wq // width)
        for k in range(PLANE):
            keep = pltpu.roll(k_in[k, c // 2], lax.rem(LANES - first, LANES), 1)
            gain = jnp.broadcast_to(keep[:, 0:1], (8, wq))
            for h in range(1, wq // width):
                gain = jnp.where(lane >= h * width, jnp.broadcast_to(keep[:, h:h + 1], (8, wq)), gain)
            gains[c, k] = gain

    def done_by(step):
        due = jnp.maximum(step + 1 - lag, 0)
        due = jnp.where(step == end - 1, by_plane(NEXT_DONE), due)
        return jnp.where(step == end, by_plane(LAST_DONE), due)

    def follow(step):
        loop(done_by(step), chain_stage, low=done_by(step - 1))
        late = by_plane(OUT_LAGS)
        loop(done_by(step) - late, output_stage, low=jnp.maximum(done_by(step - 1) - late, 0))

    def turn(g):
        for k in range(2):
            arrived(g, k)

            @pl.when(g < G - 1)
            def _():
                issue(g + 1, k)

            states_stage(g, k)
            inner_stage(g, k)
            if k == 0:
                @pl.when(g == 0)
                def _():
                    own_keep.wait()
                    for hop in range(1, PLANE):
                        send_keep(hop).wait_recv()
                    loop(chunks, widen)

            follow(2 * g + k)

    loop(G, turn)
    done = by_plane(LAST_DONE)
    sent = done - by_plane(OUT_LAGS)
    early = jnp.maximum(sent, jnp.where(z == nz - 1, end - 4, 0))
    near = jnp.where(z < nz - 1, end, end - 1)
    loop(near, chain_stage, low=done)
    loop(early, output_stage, low=sent)
    announce()
    loop(end, chain_stage, low=near)
    close_chain()
    loop(chunks, output_stage, low=early)

    most = slice(0, n - 1)
    pltpu.make_async_copy(ds.at[most], dr.at[most], ds_sem.at[0]).wait()
    for hop in range(1, PLANE):
        send_keep(hop).wait_send()

    def close(g):
        for k in range(2):
            departed(g, k)
            c = 2 * g + k
            for hop in range(1, PLANE):
                send_total(c, hop).wait_send()
                send_entering(c, hop).wait_send()

            @pl.when((z < nz - 1) & (c < end))
            def _():
                send_leave(c).wait_send()


    loop(G, close)
    loop(nz, lambda at: send_plane(at).wait_send(), low=z + 1)


def per_device(n, inputs, projections, step_sizes, log_rates, skip_gain, packing, prompt_sizes):
    tok = inputs.shape[1]
    head_count = log_rates.shape[0]
    heads = head_count // G
    states = projections.shape[0] // (2 * G)
    width = inputs.shape[0] // head_count
    part = heads // 2
    wp = part * width
    wx = heads * width
    wm = 2 * states
    wq = wp // PLANE
    slot = tok // n
    blocks = tok // BLOCK
    rows = states + 8
    nz = n // PLANE
    chunks = 2 * G
    hbm = pl.BlockSpec(memory_space=pltpu.HBM)
    dma = pltpu.SemaphoreType.DMA
    return pl.pallas_call(
        functools.partial(fused_kernel, n, heads, width, states),
        in_specs=[hbm] * 7,
        out_specs=pl.BlockSpec(memory_space=pltpu.VMEM),
        out_shape=jax.ShapeDtypeStruct((G * wx, tok), BF16),
        scratch_shapes=[
            pltpu.SMEM(prompt_sizes.shape, jnp.int32),
            pltpu.SMEM(skip_gain.shape, F32),
            pltpu.VMEM((1, head_count), F32),
            pltpu.VMEM((1, tok), jnp.int32),
            pltpu.VMEM((head_count, tok), BF16),
            pltpu.VMEM((chunks, wp, tok), BF16),
            pltpu.VMEM((G, wm, tok), BF16),
            pltpu.VMEM((tok, tok), BF16),
            pltpu.VMEM((G, n, slot, wm + wx), BF16),
            pltpu.VMEM((G, n, slot, wm + wx), BF16),
            pltpu.VMEM((n, slot, LANES), BF16),
            pltpu.VMEM((n, slot, LANES), BF16),
            pltpu.VMEM((G, blocks, BLOCK, LANES), F32),
            pltpu.VMEM((G, blocks, BLOCK, LANES), F32),
            pltpu.VMEM((G, blocks, 8, LANES), F32),
            pltpu.VMEM((blocks, head_count, BLOCK), F32),
            pltpu.VMEM((blocks, head_count, BLOCK), F32),
            pltpu.VMEM((blocks, head_count, BLOCK), F32),
            pltpu.VMEM((blocks, states, BLOCK), BF16),
            pltpu.VMEM((blocks, BLOCK, BLOCK), F32),
            pltpu.VMEM((blocks, BLOCK, BLOCK), F32),
            pltpu.VMEM((chunks, wp, tok), F32),
            pltpu.VMEM((chunks, states, wp), F32),
            pltpu.VMEM((chunks, blocks - 1, rows, wp), F32),
            pltpu.VMEM((chunks, PLANE, states, wq), F32),
            pltpu.VMEM((chunks, states, wq), F32),
            pltpu.VMEM((chunks, states, wq), F32),
            pltpu.VMEM((chunks, PLANE, states, wq), F32),
            pltpu.VMEM((chunks, PLANE, states, wq), F32),
            pltpu.VMEM((G, 8, LANES), F32),
            pltpu.VMEM((PLANE, G, 8, LANES), F32),
            pltpu.VMEM((chunks, PLANE, 8, wq), F32),
            pltpu.VMEM((states + 8, wq), F32),
            pltpu.VMEM((nz, states + 8, wq), F32),
            dma((2, chunks)),
            dma((5,)),
            dma((1,)),
            dma((1,)),
            dma((G, 2)),
            dma((G, 2)),
            dma((chunks, PLANE)),
            dma((chunks, PLANE)),
            dma((chunks,)),
            dma((chunks,)),
            dma((chunks, PLANE)),
            dma((chunks, PLANE)),
            dma((PLANE,)),
            dma((PLANE,)),
            dma((nz,)),
            dma((nz,)),
        ],
        compiler_params=pltpu.CompilerParams(
            collective_id=0, has_side_effects=True, vmem_limit_bytes=VLIM),
        name="prefill",
    )(*[pltpu.with_memory_space_constraint(part_, pltpu.HBM) for part_ in (
        prompt_sizes, skip_gain, log_rates.reshape(1, head_count), packing,
        inputs, projections, step_sizes)])


def solution(mesh):
    in_specs = (
        P(None, ("groups", "ctx")),
        P(None, ("groups", "ctx")),
        P(None, ("groups", "ctx")),
        P(),
        P(),
        P(("groups", "ctx"), None),
        P("groups"),
    )
    out_specs = P(None, ("groups", "ctx"))
    return jax.shard_map(
        functools.partial(per_device, mesh.shape["ctx"]),
        mesh=mesh, in_specs=in_specs, out_specs=out_specs, check_vma=False,
    )
```

```python
import functools
import jax
import jax.numpy as jnp
from jax import lax
from jax.experimental import pallas as pl
from jax.experimental.pallas import tpu as pltpu
from jax.sharding import PartitionSpec as P

G = 4
BLOCK = 128
LANES = 128
PLANE = 4
LAGS = (1,2,4,5)
LAST_DONE = (7,6,4,3)
NEXT_DONE = (7, 6, 3, 2)
OUT_LAGS = (1,1,2,2)
VLIM = 36 * 1024 * 1024
F32 = jnp.float32
BF16 = jnp.bfloat16
MESH = pl.DeviceIdType.MESH


def dot_nt(a, b):
    return lax.dot_general(a, b, (((1,), (1,)), ((), ())), preferred_element_type=F32)


def starts_of(sizes_ref):
    out = []
    at = jnp.int32(0)
    for s in range(sizes_ref.shape[0]):
        out.append(at)
        at = at + sizes_ref[s]
    return out


def segment_of(position, starts):
    seg = jnp.zeros(position.shape, jnp.int32)
    for at in starts:
        seg = seg + (position >= at).astype(jnp.int32)
    return seg


def decay_of(dt, rate):
    t = dt.shape[0]
    tri = jnp.where(
        lax.broadcasted_iota(jnp.int32, (t, t), 0) >= lax.broadcasted_iota(jnp.int32, (t, t), 1),
        1.0, 0.0).astype(F32)
    return jnp.dot(tri, dt * rate, preferred_element_type=F32, precision=lax.Precision.HIGHEST)


def spread(value, heads, width):
    rows = value.shape[0]
    per = LANES // width
    lane = lax.broadcasted_iota(jnp.int32, (rows, LANES), 1)
    out = []
    for q in range(heads // per):
        acc = jnp.broadcast_to(value[:, q * per:q * per + 1], (rows, LANES))
        for k in range(1, per):
            other = jnp.broadcast_to(value[:, q * per + k:q * per + k + 1], (rows, LANES))
            acc = jnp.where(lane >= k * width, other, acc)
        out.append(acc)
    return jnp.concatenate(out, axis=1)


def fused_kernel(
    n, heads, width, states,
    sizes_hbm, skip_hbm, rate_hbm, pack_hbm, x_hbm, bc_hbm, dt_hbm, o_ref,
    sizes_ref, skip_ref, rate_ref, pack_ref, dt_ref,
    xv, bv, pick, ys, yr, ds, dr,
    cum_g, into_g, keep_g, cum_t, dt_t, opens, maps_t, gram, allow, acc,
    t_own, t0, t_in, enter, leave, out_e, carry, k_own, k_in, gains, p_own, p_in,
    in_sem, few_sem, ds_sem, dr_sem, ys_sem, yr_sem,
    ts_sem, tr_sem, es_sem, er_sem, cs_sem, cr_sem, ks_sem, kr_sem, ps_sem, pr_sem,
):
    me = lax.axis_index("ctx")
    tok = dt_ref.shape[1]
    slot = tok // n
    part = heads // 2
    wp = part * width
    wx = heads * width
    wm = 2 * states
    wq = wp // PLANE
    chunks = 2 * G
    blocks = tok // BLOCK
    half = n // 2
    q = lax.rem(me, PLANE)
    z = me // PLANE
    nz = n // PLANE
    base = me * tok

    def by_plane(values):
        return jnp.where(z == 0, values[0], jnp.where(
            z < nz // 2, values[1], jnp.where(z < nz - 1, values[2], values[3])))

    lag = by_plane(LAGS)

    def loop(count, body, low=0):
        def step(i, _):
            body(i)
            return 0
        lax.fori_loop(low, count, step, 0)

    def load_x(c):
        r = pl.ds(pl.multiple_of(c * wp, LANES), wp)
        return pltpu.make_async_copy(x_hbm.at[r], xv.at[c], in_sem.at[0, c])

    def load_m(g):
        r = pl.ds(pl.multiple_of(g * wm, LANES), wm)
        return pltpu.make_async_copy(bc_hbm.at[r], bv.at[g], in_sem.at[1, g])

    few = [
        pltpu.make_async_copy(src, dst, few_sem.at[i])
        for i, (src, dst) in enumerate((
            (pack_hbm, pack_ref), (dt_hbm, dt_ref), (sizes_hbm, sizes_ref),
            (skip_hbm, skip_ref), (rate_hbm, rate_ref)))
    ]
    few[0].start()
    few[1].start()
    load_m(0).start()
    load_x(0).start()
    load_x(1).start()

    barrier = pltpu.get_barrier_semaphore()
    loop(n, lambda off: pl.semaphore_signal(
        barrier, inc=1, device_id={"ctx": lax.rem(me + off, n)}, device_id_type=MESH), low=1)

    for copy in few[2:]:
        copy.start()
    loop(G, lambda g: load_m(g).start(), low=1)
    loop(chunks, lambda c: load_x(c).start(), low=2)
    few[0].wait()

    rows = lax.broadcasted_iota(jnp.int32, (tok, tok), 0)
    pick[...] = jnp.where(rows == pack_ref[...], 1.0, 0.0).astype(F32).T.astype(BF16)
    head_count = dt_ref.shape[0]
    few[1].wait()
    dt_all = dot_nt(pick[...], dt_ref[...]).astype(BF16)
    dt_all = jnp.concatenate([dt_all, jnp.zeros((tok, LANES - head_count), BF16)], axis=1)
    ds[...] = dt_all.reshape(n, slot, LANES)

    def lanes_of(k):
        return slice(0, wm + wp) if k == 0 else slice(wm + wp, wm + wx)

    def prep(g, k):
        if k == 0:
            load_m(g).wait()
            ys[g, :, :, :wm] = dot_nt(pick[...], bv[g]).astype(BF16).reshape(n, slot, wm)
        load_x(2 * g + k).wait()
        y = dot_nt(pick[...], xv[2 * g + k]).astype(BF16)
        ys[g, :, :, wm + k * wp:wm + (k + 1) * wp] = y.reshape(n, slot, wp)

    def send_y(g, k, off):
        to = lax.rem(me + off, n)
        s = lanes_of(k)
        return pltpu.make_async_remote_copy(
            ys.at[g, to, :, s], yr.at[g, me, :, s], ys_sem.at[g, k], yr_sem.at[g, k],
            device_id={"ctx": to}, device_id_type=MESH)

    def send_d(off):
        to = lax.rem(me + off, n)
        return pltpu.make_async_remote_copy(
            ds.at[to], dr.at[me], ds_sem.at[0], dr_sem.at[0],
            device_id={"ctx": to}, device_id_type=MESH)

    def spread_out(send):
        def pick_off(i):
            return 1 + lax.rem(2 * n - PLANE - 1 - i, n - 1)

        def tell(i, last):
            off = pick_off(i)
            there = lax.rem(me + off, n) // PLANE == nz - 1

            @pl.when(there if last else jnp.logical_not(there))
            def _():
                send(off).start()

        loop(n, lambda i: tell(i, False), low=1)
        loop(n, lambda i: tell(i, True), low=1)

    def issue(g, k):
        s = lanes_of(k)
        spread_out(lambda off: send_y(g, k, off))
        pltpu.make_async_copy(ys.at[g, me, :, s], yr.at[g, me, :, s], yr_sem.at[g, k]).start()

    def arrived(g, k):
        s = lanes_of(k)
        pltpu.make_async_copy(ys.at[g, :, :, s], yr.at[g, :, :, s], yr_sem.at[g, k]).wait()

    def departed(g, k):
        s = lanes_of(k)
        most = slice(0, n - 1)
        pltpu.make_async_copy(ys.at[g, most, :, s], yr.at[g, most, :, s], ys_sem.at[g, k]).wait()

    prep(0, 0)
    pl.semaphore_wait(barrier, n - 1)
    spread_out(send_d)
    pltpu.make_async_copy(ds.at[me], dr.at[me], dr_sem.at[0]).start()
    issue(0, 0)
    prep(0, 1)
    issue(0, 1)

    def prep_rest(g):
        prep(g, 0)
        prep(g, 1)

    loop(G, prep_rest, low=1)

    for copy in few[2:]:
        copy.wait()
    starts = starts_of(sizes_ref)
    rate = jnp.concatenate(
        [rate_ref[...], jnp.zeros((1, LANES - head_count), F32)], axis=1)
    rate = jnp.broadcast_to(-jnp.exp(rate), (8, LANES))[0:1]

    pltpu.make_async_copy(ds, dr, dr_sem.at[0]).wait()

    def rows_of(b):
        return slice(b * BLOCK // slot, (b + 1) * BLOCK // slot)

    for b in range(blocks):
        head = base + b * BLOCK
        last = head + BLOCK - 1
        dt = dr[rows_of(b)].reshape(BLOCK, LANES).astype(F32)
        cum = decay_of(dt, rate)
        end = cum[BLOCK - 1:BLOCK, :]
        pos = head + lax.broadcasted_iota(jnp.int32, (BLOCK, LANES), 0)
        last_seg = jnp.int32(0)
        cut = jnp.int32(0)
        for at in starts:
            last_seg = last_seg + (last >= at).astype(jnp.int32)
            cut = cut + ((at >= head) & (at <= last)).astype(jnp.int32)
        same = segment_of(pos, starts) == last_seg
        into = jnp.where(same, jnp.exp(end - cum), 0.0) * dt
        keep = jnp.broadcast_to(jnp.where(cut == 0, jnp.exp(end), 0.0), (8, LANES))
        for g in range(G):
            shift = (LANES - g * heads) % LANES
            cum_g[g, b] = pltpu.roll(cum, shift, 1)
            into_g[g, b] = pltpu.roll(into, shift, 1)
            keep_g[g, b] = pltpu.roll(keep, shift, 1)
        across = cum.T[:head_count]
        cum_t[b] = across
        dt_t[b] = dt.T[:head_count]
        row_pos = head + lax.broadcasted_iota(jnp.int32, (1, BLOCK), 1)
        row_cut = jnp.zeros((1, BLOCK), jnp.int32)
        for at in starts:
            row_cut = row_cut + ((row_pos >= at) & (at >= head)).astype(jnp.int32)
        opens[b] = jnp.where(row_cut == 0, jnp.exp(across), 0.0)
        pos_i = head + lax.broadcasted_iota(jnp.int32, (BLOCK, BLOCK), 0)
        pos_j = head + lax.broadcasted_iota(jnp.int32, (BLOCK, BLOCK), 1)
        fits = (pos_i >= pos_j) & (segment_of(pos_i, starts) == segment_of(pos_j, starts))
        allow[b] = jnp.where(fits, 0.0, -jnp.inf)

    for g in range(G):
        keep = keep_g[g, 0]
        for b in range(1, blocks):
            keep = keep * keep_g[g, b]
        k_own[g] = keep

    def send_keep(hop):
        return pltpu.make_async_remote_copy(
            k_own, k_in.at[q], ks_sem.at[hop], kr_sem.at[hop],
            device_id={"ctx": z * PLANE + lax.rem(q + hop, PLANE)}, device_id_type=MESH)

    own_keep = pltpu.make_async_copy(k_own, k_in.at[q], kr_sem.at[0])
    for hop in range(1, PLANE):
        send_keep(hop).start()
    own_keep.start()

    def y_of(g, b, lo, hi):
        return yr[g, rows_of(b), :, lo:hi].reshape(BLOCK, hi - lo)

    def x_of(g, k, b):
        return y_of(g, b, wm + k * wp, wm + (k + 1) * wp)

    def quarter(k):
        return slice(k * wq, (k + 1) * wq)

    def send_total(c, hop):
        to = lax.rem(q + hop, PLANE)
        s = pl.ds(pl.multiple_of(to * wq, LANES), wq)
        return pltpu.make_async_remote_copy(
            t_own.at[c, :, s], t_in.at[c, q], ts_sem.at[c, hop], tr_sem.at[c, hop],
            device_id={"ctx": z * PLANE + to}, device_id_type=MESH)

    def own_total(c):
        s = pl.ds(pl.multiple_of(q * wq, LANES), wq)
        return pltpu.make_async_copy(t_own.at[c, :, s], t_in.at[c, q], tr_sem.at[c, 0])

    def send_leave(c):
        return pltpu.make_async_remote_copy(
            leave.at[c], enter.at[c], es_sem.at[c], er_sem.at[c],
            device_id={"ctx": me + PLANE}, device_id_type=MESH)

    def take_enter(c):
        return pltpu.make_async_remote_copy(
            leave.at[c], enter.at[c], es_sem.at[c], er_sem.at[c],
            device_id={"ctx": me - PLANE}, device_id_type=MESH)

    def send_entering(c, hop):
        to = lax.rem(q + hop, PLANE)
        return pltpu.make_async_remote_copy(
            out_e.at[c, to], carry.at[c, q], cs_sem.at[c, hop], cr_sem.at[c, hop],
            device_id={"ctx": z * PLANE + to}, device_id_type=MESH)

    def own_entering(c):
        return pltpu.make_async_copy(out_e.at[c, q], carry.at[c, q], cr_sem.at[c, 0])

    def states_stage(g, k):
        c = 2 * g + k
        total = None
        for b in range(blocks):
            if k == 0:
                in_map = y_of(g, b, 0, states)
                out_map = y_of(g, b, states, wm)
                maps_t[b] = in_map.astype(F32).T.astype(BF16)
                gram[b] = dot_nt(out_map, in_map)
            cols = slice(k * part, (k + 1) * part)
            into = spread(into_g[g, b][:, cols], part, width)
            weighted = (x_of(g, k, b).astype(F32) * into).astype(BF16)
            block_total = jnp.dot(maps_t[b], weighted, preferred_element_type=F32)
            keep = spread(keep_g[g, b][:, cols], part, width)
            if total is None:
                total = block_total
            else:
                total = keep[0:1] * total + block_total
            if b < blocks - 1:
                t0[c, b, :states, :] = block_total
                t0[c, b, states:, :] = keep
        t_own[c] = total
        for hop in range(1, PLANE):
            send_total(c, hop).start()
        own_total(c).start()

    def inner_stage(g, k):
        c = 2 * g + k
        first = pl.multiple_of(c * part, part)
        for b in range(blocks):
            lo = b * BLOCK
            cum = cum_g[g, b]
            across = cum_t[b, pl.ds(first, part), :]
            dt = dt_t[b, pl.ds(first, part), :]
            x_fm = x_of(g, k, b).T
            for h in range(part):
                col = k * part + h
                gap = jnp.broadcast_to(cum[:, col:col + 1], (BLOCK, BLOCK)) - across[h:h + 1]
                mask = jnp.exp(gap + allow[b])
                mixing = (gram[b] * (mask * dt[h:h + 1])).astype(BF16)
                r = slice(h * width, (h + 1) * width)
                xh = x_fm[r]
                acc[c, r, lo:lo + BLOCK] = (
                    dot_nt(xh, mixing) + skip_ref[c * part + h] * xh.astype(F32))

    end = chunks - 1

    def totals_in(c):
        for hop in range(1, PLANE):
            send_total(c, hop).wait_recv()
        own_total(c).wait()

    def hand_out(c, state):
        for k in range(PLANE):
            out_e[c, k] = state
            if k < PLANE - 1:
                state = gains[c, k, 0:1] * state + t_in[c, k]
        for hop in range(1, PLANE):
            send_entering(c, hop).start()
        own_entering(c).start()

    def chain_stage(c):
        totals_in(c)

        @pl.when(z > 0)
        def _():
            take_enter(c).wait_recv()

        @pl.when(z == 0)
        def _():
            enter[c] = jnp.zeros((states, wq), F32)

        @pl.when(z < nz - 1)
        def _():
            state = enter[c]
            for k in range(PLANE):
                state = gains[c, k, 0:1] * state + t_in[c, k]
            leave[c] = state
            send_leave(c).start()

        hand_out(c, enter[c])

    def send_plane(to):
        return pltpu.make_async_remote_copy(
            p_own, p_in.at[z], ps_sem.at[to], pr_sem.at[z],
            device_id={"ctx": to * PLANE + q}, device_id_type=MESH)

    def take_plane(at):
        return pltpu.make_async_remote_copy(
            p_own, p_in.at[at], ps_sem.at[at], pr_sem.at[at],
            device_id={"ctx": at * PLANE + q}, device_id_type=MESH)

    told = jnp.where(z == 0, jnp.minimum(nz, 2), nz)

    def announce():
        totals_in(end)

        @pl.when(z < nz - 1)
        def _():
            total, gain = t_in[end, 0], gains[end, 0]
            for k in range(1, PLANE):
                total = gains[end, k, 0:1] * total + t_in[end, k]
                gain = gain * gains[end, k]
            p_own[:states] = total
            p_own[states:] = gain

            @pl.when(z == 1)
            def _():
                take_plane(0).wait_recv()
                p_own[:states] = gain[0:1] * p_in[0, :states] + total

            loop(told, lambda to: send_plane(to).start(), low=z + 1)

    def close_chain():
        enter[end] = jnp.zeros((states, wq), F32)

        def add(at):
            take_plane(at).wait_recv()
            enter[end] = p_in[at, states:states + 1] * enter[end] + p_in[at, :states]


        @pl.when(z == 1)
        def _():
            enter[end] = p_in[0, :states]

        loop(z, add, low=1)
        hand_out(end, enter[end])

    def output_stage(c):
        for hop in range(1, PLANE):
            send_entering(c, hop).wait_recv()
        own_entering(c).wait()
        g = c // 2
        first = pl.multiple_of(c * part, part)
        state = jnp.concatenate([carry[c, k] for k in range(PLANE)], axis=1)
        for b in range(blocks):
            lo = b * BLOCK
            out_map = y_of(g, b, states, wm)
            carried = dot_nt(state.astype(BF16).T, out_map)
            opened = opens[b, pl.ds(first, part), :]
            for h in range(part):
                r = slice(h * width, (h + 1) * width)
                o_ref[pl.ds(pl.multiple_of(c * wp + h * width, width), width), lo:lo + BLOCK] = (
                    acc[c, r, lo:lo + BLOCK] + carried[r] * opened[h:h + 1]).astype(BF16)
            if b < blocks - 1:
                state = t0[c, b, states:states + 1, :] * state + t0[c, b, :states, :]

    lane = lax.broadcasted_iota(jnp.int32, (8, wq), 1)

    def widen(c):
        first = lax.rem(c, 2) * part + q * (wq // width)
        for k in range(PLANE):
            keep = pltpu.roll(k_in[k, c // 2], lax.rem(LANES - first, LANES), 1)
            gain = jnp.broadcast_to(keep[:, 0:1], (8, wq))
            for h in range(1, wq // width):
                gain = jnp.where(lane >= h * width, jnp.broadcast_to(keep[:, h:h + 1], (8, wq)), gain)
            gains[c, k] = gain

    def done_by(step):
        due = jnp.maximum(step + 1 - lag, 0)
        due = jnp.where(step == end - 1, by_plane(NEXT_DONE), due)
        return jnp.where(step == end, by_plane(LAST_DONE), due)

    def follow(step):
        loop(done_by(step), chain_stage, low=done_by(step - 1))
        late = by_plane(OUT_LAGS)
        loop(done_by(step) - late, output_stage, low=jnp.maximum(done_by(step - 1) - late, 0))

    def turn(g):
        for k in range(2):
            arrived(g, k)

            @pl.when(g < G - 1)
            def _():
                issue(g + 1, k)

            states_stage(g, k)
            inner_stage(g, k)
            if k == 0:
                @pl.when(g == 0)
                def _():
                    own_keep.wait()
                    for hop in range(1, PLANE):
                        send_keep(hop).wait_recv()
                    loop(chunks, widen)

            follow(2 * g + k)

    loop(G, turn)
    done = by_plane(LAST_DONE)
    sent = done - by_plane(OUT_LAGS)
    early = jnp.maximum(sent, jnp.where(z == nz - 1, end - 4, 0))
    near = jnp.where(z < nz - 1, end, end - 1)
    loop(near, chain_stage, low=done)
    loop(early, output_stage, low=sent)
    announce()
    loop(end, chain_stage, low=near)
    close_chain()
    loop(chunks, output_stage, low=early)

    most = slice(0, n - 1)
    pltpu.make_async_copy(ds.at[most], dr.at[most], ds_sem.at[0]).wait()
    for hop in range(1, PLANE):
        send_keep(hop).wait_send()

    def close(g):
        for k in range(2):
            departed(g, k)
            c = 2 * g + k
            for hop in range(1, PLANE):
                send_total(c, hop).wait_send()
                send_entering(c, hop).wait_send()

            @pl.when((z < nz - 1) & (c < end))
            def _():
                send_leave(c).wait_send()


    loop(G, close)
    loop(told, lambda to: send_plane(to).wait_send(), low=z + 1)


def per_device(n, inputs, projections, step_sizes, log_rates, skip_gain, packing, prompt_sizes):
    tok = inputs.shape[1]
    head_count = log_rates.shape[0]
    heads = head_count // G
    states = projections.shape[0] // (2 * G)
    width = inputs.shape[0] // head_count
    part = heads // 2
    wp = part * width
    wx = heads * width
    wm = 2 * states
    wq = wp // PLANE
    slot = tok // n
    blocks = tok // BLOCK
    rows = states + 8
    nz = n // PLANE
    chunks = 2 * G
    hbm = pl.BlockSpec(memory_space=pltpu.HBM)
    dma = pltpu.SemaphoreType.DMA
    return pl.pallas_call(
        functools.partial(fused_kernel, n, heads, width, states),
        in_specs=[hbm] * 7,
        out_specs=pl.BlockSpec(memory_space=pltpu.VMEM),
        out_shape=jax.ShapeDtypeStruct((G * wx, tok), BF16),
        scratch_shapes=[
            pltpu.SMEM(prompt_sizes.shape, jnp.int32),
            pltpu.SMEM(skip_gain.shape, F32),
            pltpu.VMEM((1, head_count), F32),
            pltpu.VMEM((1, tok), jnp.int32),
            pltpu.VMEM((head_count, tok), BF16),
            pltpu.VMEM((chunks, wp, tok), BF16),
            pltpu.VMEM((G, wm, tok), BF16),
            pltpu.VMEM((tok, tok), BF16),
            pltpu.VMEM((G, n, slot, wm + wx), BF16),
            pltpu.VMEM((G, n, slot, wm + wx), BF16),
            pltpu.VMEM((n, slot, LANES), BF16),
            pltpu.VMEM((n, slot, LANES), BF16),
            pltpu.VMEM((G, blocks, BLOCK, LANES), F32),
            pltpu.VMEM((G, blocks, BLOCK, LANES), F32),
            pltpu.VMEM((G, blocks, 8, LANES), F32),
            pltpu.VMEM((blocks, head_count, BLOCK), F32),
            pltpu.VMEM((blocks, head_count, BLOCK), F32),
            pltpu.VMEM((blocks, head_count, BLOCK), F32),
            pltpu.VMEM((blocks, states, BLOCK), BF16),
            pltpu.VMEM((blocks, BLOCK, BLOCK), F32),
            pltpu.VMEM((blocks, BLOCK, BLOCK), F32),
            pltpu.VMEM((chunks, wp, tok), F32),
            pltpu.VMEM((chunks, states, wp), F32),
            pltpu.VMEM((chunks, blocks - 1, rows, wp), F32),
            pltpu.VMEM((chunks, PLANE, states, wq), F32),
            pltpu.VMEM((chunks, states, wq), F32),
            pltpu.VMEM((chunks, states, wq), F32),
            pltpu.VMEM((chunks, PLANE, states, wq), F32),
            pltpu.VMEM((chunks, PLANE, states, wq), F32),
            pltpu.VMEM((G, 8, LANES), F32),
            pltpu.VMEM((PLANE, G, 8, LANES), F32),
            pltpu.VMEM((chunks, PLANE, 8, wq), F32),
            pltpu.VMEM((states + 8, wq), F32),
            pltpu.VMEM((nz, states + 8, wq), F32),
            dma((2, chunks)),
            dma((5,)),
            dma((1,)),
            dma((1,)),
            dma((G, 2)),
            dma((G, 2)),
            dma((chunks, PLANE)),
            dma((chunks, PLANE)),
            dma((chunks,)),
            dma((chunks,)),
            dma((chunks, PLANE)),
            dma((chunks, PLANE)),
            dma((PLANE,)),
            dma((PLANE,)),
            dma((nz,)),
            dma((nz,)),
        ],
        compiler_params=pltpu.CompilerParams(
            collective_id=0, has_side_effects=True, vmem_limit_bytes=VLIM),
        name="prefill",
    )(*[pltpu.with_memory_space_constraint(part_, pltpu.HBM) for part_ in (
        prompt_sizes, skip_gain, log_rates.reshape(1, head_count), packing,
        inputs, projections, step_sizes)])


def solution(mesh):
    in_specs = (
        P(None, ("groups", "ctx")),
        P(None, ("groups", "ctx")),
        P(None, ("groups", "ctx")),
        P(),
        P(),
        P(("groups", "ctx"), None),
        P("groups"),
    )
    out_specs = P(None, ("groups", "ctx"))
    return jax.shard_map(
        functools.partial(per_device, mesh.shape["ctx"]),
        mesh=mesh, in_specs=in_specs, out_specs=out_specs, check_vma=False,
    )
```

```python
import functools
import jax
import jax.numpy as jnp
from jax import lax
from jax.experimental import pallas as pl
from jax.experimental.pallas import tpu as pltpu
from jax.sharding import PartitionSpec as P

G = 4
BLOCK = 128
LANES = 128
PLANE = 4
LAGS = (1,2,4,5)
LAST_DONE = (7,6,4,3)
NEXT_DONE = (7, 6, 3, 2)
OUT_LAGS = (1,1,2,2)
VLIM = 36 * 1024 * 1024
F32 = jnp.float32
BF16 = jnp.bfloat16
MESH = pl.DeviceIdType.MESH


def dot_nt(a, b):
    return lax.dot_general(a, b, (((1,), (1,)), ((), ())), preferred_element_type=F32)


def starts_of(sizes_ref):
    out = []
    at = jnp.int32(0)
    for s in range(sizes_ref.shape[0]):
        out.append(at)
        at = at + sizes_ref[s]
    return out


def segment_of(position, starts):
    seg = jnp.zeros(position.shape, jnp.int32)
    for at in starts:
        seg = seg + (position >= at).astype(jnp.int32)
    return seg


def decay_of(dt, rate):
    t = dt.shape[0]
    tri = jnp.where(
        lax.broadcasted_iota(jnp.int32, (t, t), 0) >= lax.broadcasted_iota(jnp.int32, (t, t), 1),
        1.0, 0.0).astype(F32)
    return jnp.dot(tri, dt * rate, preferred_element_type=F32, precision=lax.Precision.HIGHEST)


def spread(value, heads, width):
    rows = value.shape[0]
    per = LANES // width
    lane = lax.broadcasted_iota(jnp.int32, (rows, LANES), 1)
    out = []
    for q in range(heads // per):
        acc = jnp.broadcast_to(value[:, q * per:q * per + 1], (rows, LANES))
        for k in range(1, per):
            other = jnp.broadcast_to(value[:, q * per + k:q * per + k + 1], (rows, LANES))
            acc = jnp.where(lane >= k * width, other, acc)
        out.append(acc)
    return jnp.concatenate(out, axis=1)


def fused_kernel(
    n, heads, width, states,
    sizes_hbm, skip_hbm, rate_hbm, pack_hbm, x_hbm, bc_hbm, dt_hbm, o_ref,
    sizes_ref, skip_ref, rate_ref, pack_ref, dt_ref,
    xv, bv, pick, ys, yr, ds, dr,
    cum_g, into_g, keep_g, cum_t, dt_t, opens, maps_t, gram, allow, acc,
    t_own, t0, t_in, enter, leave, out_e, carry, k_own, k_in, gains, p_own, p_in,
    in_sem, few_sem, ds_sem, dr_sem, ys_sem, yr_sem,
    ts_sem, tr_sem, es_sem, er_sem, cs_sem, cr_sem, ks_sem, kr_sem, ps_sem, pr_sem,
):
    me = lax.axis_index("ctx")
    tok = dt_ref.shape[1]
    slot = tok // n
    part = heads // 2
    wp = part * width
    wx = heads * width
    wm = 2 * states
    wq = wp // PLANE
    chunks = 2 * G
    blocks = tok // BLOCK
    half = n // 2
    q = lax.rem(me, PLANE)
    z = me // PLANE
    nz = n // PLANE
    base = me * tok

    def by_plane(values):
        return jnp.where(z == 0, values[0], jnp.where(
            z < nz // 2, values[1], jnp.where(z < nz - 1, values[2], values[3])))

    lag = by_plane(LAGS)

    def loop(count, body, low=0):
        def step(i, _):
            body(i)
            return 0
        lax.fori_loop(low, count, step, 0)

    def load_x(c):
        r = pl.ds(pl.multiple_of(c * wp, LANES), wp)
        return pltpu.make_async_copy(x_hbm.at[r], xv.at[c], in_sem.at[0, c])

    def load_m(g):
        r = pl.ds(pl.multiple_of(g * wm, LANES), wm)
        return pltpu.make_async_copy(bc_hbm.at[r], bv.at[g], in_sem.at[1, g])

    few = [
        pltpu.make_async_copy(src, dst, few_sem.at[i])
        for i, (src, dst) in enumerate((
            (pack_hbm, pack_ref), (dt_hbm, dt_ref), (sizes_hbm, sizes_ref),
            (skip_hbm, skip_ref), (rate_hbm, rate_ref)))
    ]
    few[0].start()
    few[1].start()
    load_m(0).start()
    load_x(0).start()
    load_x(1).start()

    barrier = pltpu.get_barrier_semaphore()
    loop(n, lambda off: pl.semaphore_signal(
        barrier, inc=1, device_id={"ctx": lax.rem(me + off, n)}, device_id_type=MESH), low=1)

    for copy in few[2:]:
        copy.start()
    loop(G, lambda g: load_m(g).start(), low=1)
    loop(chunks, lambda c: load_x(c).start(), low=2)
    few[0].wait()

    rows = lax.broadcasted_iota(jnp.int32, (tok, tok), 0)
    pick[...] = jnp.where(rows == pack_ref[...], 1.0, 0.0).astype(F32).T.astype(BF16)
    head_count = dt_ref.shape[0]
    few[1].wait()
    dt_all = dot_nt(pick[...], dt_ref[...]).astype(BF16)
    dt_all = jnp.concatenate([dt_all, jnp.zeros((tok, LANES - head_count), BF16)], axis=1)
    ds[...] = dt_all.reshape(n, slot, LANES)

    def lanes_of(k):
        return slice(0, wm + wp) if k == 0 else slice(wm + wp, wm + wx)

    def prep(g, k):
        if k == 0:
            load_m(g).wait()
            ys[g, :, :, :wm] = dot_nt(pick[...], bv[g]).astype(BF16).reshape(n, slot, wm)
        load_x(2 * g + k).wait()
        y = dot_nt(pick[...], xv[2 * g + k]).astype(BF16)
        ys[g, :, :, wm + k * wp:wm + (k + 1) * wp] = y.reshape(n, slot, wp)

    def send_y(g, k, off):
        to = lax.rem(me + off, n)
        s = lanes_of(k)
        return pltpu.make_async_remote_copy(
            ys.at[g, to, :, s], yr.at[g, me, :, s], ys_sem.at[g, k], yr_sem.at[g, k],
            device_id={"ctx": to}, device_id_type=MESH)

    def send_d(off):
        to = lax.rem(me + off, n)
        return pltpu.make_async_remote_copy(
            ds.at[to], dr.at[me], ds_sem.at[0], dr_sem.at[0],
            device_id={"ctx": to}, device_id_type=MESH)

    def spread_out(send):
        def pick_off(i):
            return 1 + lax.rem(2 * n - PLANE - 1 - i, n - 1)

        def tell(i, last):
            off = pick_off(i)
            there = lax.rem(me + off, n) // PLANE == nz - 1

            @pl.when(there if last else jnp.logical_not(there))
            def _():
                send(off).start()

        loop(n, lambda i: tell(i, False), low=1)
        loop(n, lambda i: tell(i, True), low=1)

    def issue(g, k):
        s = lanes_of(k)
        spread_out(lambda off: send_y(g, k, off))
        pltpu.make_async_copy(ys.at[g, me, :, s], yr.at[g, me, :, s], yr_sem.at[g, k]).start()

    def arrived(g, k):
        s = lanes_of(k)
        pltpu.make_async_copy(ys.at[g, :, :, s], yr.at[g, :, :, s], yr_sem.at[g, k]).wait()

    def departed(g, k):
        s = lanes_of(k)
        most = slice(0, n - 1)
        pltpu.make_async_copy(ys.at[g, most, :, s], yr.at[g, most, :, s], ys_sem.at[g, k]).wait()

    prep(0, 0)
    pl.semaphore_wait(barrier, n - 1)
    spread_out(send_d)
    pltpu.make_async_copy(ds.at[me], dr.at[me], dr_sem.at[0]).start()
    issue(0, 0)
    prep(0, 1)
    issue(0, 1)

    def prep_rest(g):
        prep(g, 0)
        prep(g, 1)

    loop(G, prep_rest, low=1)

    for copy in few[2:]:
        copy.wait()
    starts = starts_of(sizes_ref)
    rate = jnp.concatenate(
        [rate_ref[...], jnp.zeros((1, LANES - head_count), F32)], axis=1)
    rate = jnp.broadcast_to(-jnp.exp(rate), (8, LANES))[0:1]

    pltpu.make_async_copy(ds, dr, dr_sem.at[0]).wait()

    def rows_of(b):
        return slice(b * BLOCK // slot, (b + 1) * BLOCK // slot)

    for b in range(blocks):
        head = base + b * BLOCK
        last = head + BLOCK - 1
        dt = dr[rows_of(b)].reshape(BLOCK, LANES).astype(F32)
        cum = decay_of(dt, rate)
        end = cum[BLOCK - 1:BLOCK, :]
        pos = head + lax.broadcasted_iota(jnp.int32, (BLOCK, LANES), 0)
        last_seg = jnp.int32(0)
        cut = jnp.int32(0)
        for at in starts:
            last_seg = last_seg + (last >= at).astype(jnp.int32)
            cut = cut + ((at >= head) & (at <= last)).astype(jnp.int32)
        same = segment_of(pos, starts) == last_seg
        into = jnp.where(same, jnp.exp(end - cum), 0.0) * dt
        keep = jnp.broadcast_to(jnp.where(cut == 0, jnp.exp(end), 0.0), (8, LANES))
        for g in range(G):
            shift = (LANES - g * heads) % LANES
            cum_g[g, b] = pltpu.roll(cum, shift, 1)
            into_g[g, b] = pltpu.roll(into, shift, 1)
            keep_g[g, b] = pltpu.roll(keep, shift, 1)
        across = cum.T[:head_count]
        cum_t[b] = across
        dt_t[b] = dt.T[:head_count]
        row_pos = head + lax.broadcasted_iota(jnp.int32, (1, BLOCK), 1)
        row_cut = jnp.zeros((1, BLOCK), jnp.int32)
        for at in starts:
            row_cut = row_cut + ((row_pos >= at) & (at >= head)).astype(jnp.int32)
        opens[b] = jnp.where(row_cut == 0, jnp.exp(across), 0.0)
        pos_i = head + lax.broadcasted_iota(jnp.int32, (BLOCK, BLOCK), 0)
        pos_j = head + lax.broadcasted_iota(jnp.int32, (BLOCK, BLOCK), 1)
        fits = (pos_i >= pos_j) & (segment_of(pos_i, starts) == segment_of(pos_j, starts))
        allow[b] = jnp.where(fits, 0.0, -jnp.inf)

    for g in range(G):
        keep = keep_g[g, 0]
        for b in range(1, blocks):
            keep = keep * keep_g[g, b]
        k_own[g] = keep

    def send_keep(hop):
        return pltpu.make_async_remote_copy(
            k_own, k_in.at[q], ks_sem.at[hop], kr_sem.at[hop],
            device_id={"ctx": z * PLANE + lax.rem(q + hop, PLANE)}, device_id_type=MESH)

    own_keep = pltpu.make_async_copy(k_own, k_in.at[q], kr_sem.at[0])
    for hop in range(1, PLANE):
        send_keep(hop).start()
    own_keep.start()

    def y_of(g, b, lo, hi):
        return yr[g, rows_of(b), :, lo:hi].reshape(BLOCK, hi - lo)

    def x_of(g, k, b):
        return y_of(g, b, wm + k * wp, wm + (k + 1) * wp)

    def quarter(k):
        return slice(k * wq, (k + 1) * wq)

    def send_total(c, hop):
        to = lax.rem(q + hop, PLANE)
        s = pl.ds(pl.multiple_of(to * wq, LANES), wq)
        return pltpu.make_async_remote_copy(
            t_own.at[c, :, s], t_in.at[c, q], ts_sem.at[c, hop], tr_sem.at[c, hop],
            device_id={"ctx": z * PLANE + to}, device_id_type=MESH)

    def own_total(c):
        s = pl.ds(pl.multiple_of(q * wq, LANES), wq)
        return pltpu.make_async_copy(t_own.at[c, :, s], t_in.at[c, q], tr_sem.at[c, 0])

    def send_leave(c):
        return pltpu.make_async_remote_copy(
            leave.at[c], enter.at[c], es_sem.at[c], er_sem.at[c],
            device_id={"ctx": me + PLANE}, device_id_type=MESH)

    def take_enter(c):
        return pltpu.make_async_remote_copy(
            leave.at[c], enter.at[c], es_sem.at[c], er_sem.at[c],
            device_id={"ctx": me - PLANE}, device_id_type=MESH)

    def send_entering(c, hop):
        to = lax.rem(q + hop, PLANE)
        return pltpu.make_async_remote_copy(
            out_e.at[c, to], carry.at[c, q], cs_sem.at[c, hop], cr_sem.at[c, hop],
            device_id={"ctx": z * PLANE + to}, device_id_type=MESH)

    def own_entering(c):
        return pltpu.make_async_copy(out_e.at[c, q], carry.at[c, q], cr_sem.at[c, 0])

    def states_stage(g, k):
        c = 2 * g + k
        total = None
        for b in range(blocks):
            if k == 0:
                in_map = y_of(g, b, 0, states)
                out_map = y_of(g, b, states, wm)
                maps_t[b] = in_map.astype(F32).T.astype(BF16)
                gram[b] = dot_nt(out_map, in_map)
            cols = slice(k * part, (k + 1) * part)
            into = spread(into_g[g, b][:, cols], part, width)
            weighted = (x_of(g, k, b).astype(F32) * into).astype(BF16)
            block_total = jnp.dot(maps_t[b], weighted, preferred_element_type=F32)
            keep = spread(keep_g[g, b][:, cols], part, width)
            if total is None:
                total = block_total
            else:
                total = keep[0:1] * total + block_total
            if b < blocks - 1:
                t0[c, b, :states, :] = block_total
                t0[c, b, states:, :] = keep
        t_own[c] = total
        for hop in range(1, PLANE):
            send_total(c, hop).start()
        own_total(c).start()

    def inner_stage(g, k):
        c = 2 * g + k
        first = pl.multiple_of(c * part, part)
        for b in range(blocks):
            lo = b * BLOCK
            cum = cum_g[g, b]
            across = cum_t[b, pl.ds(first, part), :]
            dt = dt_t[b, pl.ds(first, part), :]
            x_fm = x_of(g, k, b).T
            for h in range(part):
                col = k * part + h
                gap = jnp.broadcast_to(cum[:, col:col + 1], (BLOCK, BLOCK)) - across[h:h + 1]
                mask = jnp.exp(gap + allow[b])
                mixing = (gram[b] * (mask * dt[h:h + 1])).astype(BF16)
                r = slice(h * width, (h + 1) * width)
                xh = x_fm[r]
                acc[c, r, lo:lo + BLOCK] = (
                    dot_nt(xh, mixing) + skip_ref[c * part + h] * xh.astype(F32))

    end = chunks - 1

    def totals_in(c):
        for hop in range(1, PLANE):
            send_total(c, hop).wait_recv()
        own_total(c).wait()

    def hand_out(c, state):
        for k in range(PLANE):
            out_e[c, k] = state
            if k < PLANE - 1:
                state = gains[c, k, 0:1] * state + t_in[c, k]
        for hop in range(1, PLANE):
            send_entering(c, hop).start()
        own_entering(c).start()

    def chain_stage(c):
        totals_in(c)

        @pl.when(z > 0)
        def _():
            take_enter(c).wait_recv()

        @pl.when(z == 0)
        def _():
            enter[c] = jnp.zeros((states, wq), F32)

        @pl.when(z < nz - 1)
        def _():
            state = enter[c]
            for k in range(PLANE):
                state = gains[c, k, 0:1] * state + t_in[c, k]
            leave[c] = state
            send_leave(c).start()

        hand_out(c, enter[c])

    def send_plane(to):
        return pltpu.make_async_remote_copy(
            p_own, p_in.at[z], ps_sem.at[to], pr_sem.at[z],
            device_id={"ctx": to * PLANE + q}, device_id_type=MESH)

    def take_plane(at):
        return pltpu.make_async_remote_copy(
            p_own, p_in.at[at], ps_sem.at[at], pr_sem.at[at],
            device_id={"ctx": at * PLANE + q}, device_id_type=MESH)

    told = jnp.where(z == 0, jnp.minimum(nz, 2), nz)

    def announce():
        totals_in(end)

        @pl.when(z < nz - 1)
        def _():
            total, gain = t_in[end, 0], gains[end, 0]
            for k in range(1, PLANE):
                total = gains[end, k, 0:1] * total + t_in[end, k]
                gain = gain * gains[end, k]
            p_own[:states] = total
            p_own[states:] = gain

            @pl.when(z == 1)
            def _():
                take_plane(0).wait_recv()
                p_own[:states] = gain[0:1] * p_in[0, :states] + total

            loop(told, lambda to: send_plane(to).start(), low=z + 1)

    def close_chain():
        enter[end] = jnp.zeros((states, wq), F32)

        def add(at):
            take_plane(at).wait_recv()
            enter[end] = p_in[at, states:states + 1] * enter[end] + p_in[at, :states]


        @pl.when(z == 1)
        def _():
            enter[end] = p_in[0, :states]

        loop(z, add, low=1)
        hand_out(end, enter[end])

    def output_stage(c):
        for hop in range(1, PLANE):
            send_entering(c, hop).wait_recv()
        own_entering(c).wait()
        g = c // 2
        first = pl.multiple_of(c * part, part)
        state = jnp.concatenate([carry[c, k] for k in range(PLANE)], axis=1)
        for b in range(blocks):
            lo = b * BLOCK
            out_map = y_of(g, b, states, wm)
            carried = dot_nt(state.astype(BF16).T, out_map)
            opened = opens[b, pl.ds(first, part), :]
            for h in range(part):
                r = slice(h * width, (h + 1) * width)
                o_ref[pl.ds(pl.multiple_of(c * wp + h * width, width), width), lo:lo + BLOCK] = (
                    acc[c, r, lo:lo + BLOCK] + carried[r] * opened[h:h + 1]).astype(BF16)
            if b < blocks - 1:
                state = t0[c, b, states:states + 1, :] * state + t0[c, b, :states, :]

    lane = lax.broadcasted_iota(jnp.int32, (8, wq), 1)

    def widen(c):
        first = lax.rem(c, 2) * part + q * (wq // width)
        for k in range(PLANE):
            keep = pltpu.roll(k_in[k, c // 2], lax.rem(LANES - first, LANES), 1)
            gain = jnp.broadcast_to(keep[:, 0:1], (8, wq))
            for h in range(1, wq // width):
                gain = jnp.where(lane >= h * width, jnp.broadcast_to(keep[:, h:h + 1], (8, wq)), gain)
            gains[c, k] = gain

    def done_by(step):
        due = jnp.maximum(step + 1 - lag, 0)
        due = jnp.where(step == end - 1, by_plane(NEXT_DONE), due)
        return jnp.where(step == end, by_plane(LAST_DONE), due)

    def advance(step, mine):
        loop(jnp.where(mine, done_by(step), 0), chain_stage, low=done_by(step - 1))

    def emit(step):
        late = by_plane(OUT_LAGS)
        loop(done_by(step) - late, output_stage, low=jnp.maximum(done_by(step - 1) - late, 0))

    def turn(g):
        for k in range(2):
            arrived(g, k)

            @pl.when(g < G - 1)
            def _():
                issue(g + 1, k)

            states_stage(g, k)
            advance(2 * g + k, z > 0)
            inner_stage(g, k)
            if k == 0:
                @pl.when(g == 0)
                def _():
                    own_keep.wait()
                    for hop in range(1, PLANE):
                        send_keep(hop).wait_recv()
                    loop(chunks, widen)

            advance(2 * g + k, z == 0)
            emit(2 * g + k)

    loop(G, turn)
    done = by_plane(LAST_DONE)
    sent = done - by_plane(OUT_LAGS)
    early = jnp.maximum(sent, jnp.where(z == nz - 1, end - 4, 0))
    near = jnp.where(z < nz - 1, end, end - 1)
    loop(near, chain_stage, low=done)
    loop(early, output_stage, low=sent)
    announce()
    loop(end, chain_stage, low=near)
    close_chain()
    loop(chunks, output_stage, low=early)

    most = slice(0, n - 1)
    pltpu.make_async_copy(ds.at[most], dr.at[most], ds_sem.at[0]).wait()
    for hop in range(1, PLANE):
        send_keep(hop).wait_send()

    def close(g):
        for k in range(2):
            departed(g, k)
            c = 2 * g + k
            for hop in range(1, PLANE):
                send_total(c, hop).wait_send()
                send_entering(c, hop).wait_send()

            @pl.when((z < nz - 1) & (c < end))
            def _():
                send_leave(c).wait_send()


    loop(G, close)
    loop(told, lambda to: send_plane(to).wait_send(), low=z + 1)


def per_device(n, inputs, projections, step_sizes, log_rates, skip_gain, packing, prompt_sizes):
    tok = inputs.shape[1]
    head_count = log_rates.shape[0]
    heads = head_count // G
    states = projections.shape[0] // (2 * G)
    width = inputs.shape[0] // head_count
    part = heads // 2
    wp = part * width
    wx = heads * width
    wm = 2 * states
    wq = wp // PLANE
    slot = tok // n
    blocks = tok // BLOCK
    rows = states + 8
    nz = n // PLANE
    chunks = 2 * G
    hbm = pl.BlockSpec(memory_space=pltpu.HBM)
    dma = pltpu.SemaphoreType.DMA
    return pl.pallas_call(
        functools.partial(fused_kernel, n, heads, width, states),
        in_specs=[hbm] * 7,
        out_specs=pl.BlockSpec(memory_space=pltpu.VMEM),
        out_shape=jax.ShapeDtypeStruct((G * wx, tok), BF16),
        scratch_shapes=[
            pltpu.SMEM(prompt_sizes.shape, jnp.int32),
            pltpu.SMEM(skip_gain.shape, F32),
            pltpu.VMEM((1, head_count), F32),
            pltpu.VMEM((1, tok), jnp.int32),
            pltpu.VMEM((head_count, tok), BF16),
            pltpu.VMEM((chunks, wp, tok), BF16),
            pltpu.VMEM((G, wm, tok), BF16),
            pltpu.VMEM((tok, tok), BF16),
            pltpu.VMEM((G, n, slot, wm + wx), BF16),
            pltpu.VMEM((G, n, slot, wm + wx), BF16),
            pltpu.VMEM((n, slot, LANES), BF16),
            pltpu.VMEM((n, slot, LANES), BF16),
            pltpu.VMEM((G, blocks, BLOCK, LANES), F32),
            pltpu.VMEM((G, blocks, BLOCK, LANES), F32),
            pltpu.VMEM((G, blocks, 8, LANES), F32),
            pltpu.VMEM((blocks, head_count, BLOCK), F32),
            pltpu.VMEM((blocks, head_count, BLOCK), F32),
            pltpu.VMEM((blocks, head_count, BLOCK), F32),
            pltpu.VMEM((blocks, states, BLOCK), BF16),
            pltpu.VMEM((blocks, BLOCK, BLOCK), F32),
            pltpu.VMEM((blocks, BLOCK, BLOCK), F32),
            pltpu.VMEM((chunks, wp, tok), F32),
            pltpu.VMEM((chunks, states, wp), F32),
            pltpu.VMEM((chunks, blocks - 1, rows, wp), F32),
            pltpu.VMEM((chunks, PLANE, states, wq), F32),
            pltpu.VMEM((chunks, states, wq), F32),
            pltpu.VMEM((chunks, states, wq), F32),
            pltpu.VMEM((chunks, PLANE, states, wq), F32),
            pltpu.VMEM((chunks, PLANE, states, wq), F32),
            pltpu.VMEM((G, 8, LANES), F32),
            pltpu.VMEM((PLANE, G, 8, LANES), F32),
            pltpu.VMEM((chunks, PLANE, 8, wq), F32),
            pltpu.VMEM((states + 8, wq), F32),
            pltpu.VMEM((nz, states + 8, wq), F32),
            dma((2, chunks)),
            dma((5,)),
            dma((1,)),
            dma((1,)),
            dma((G, 2)),
            dma((G, 2)),
            dma((chunks, PLANE)),
            dma((chunks, PLANE)),
            dma((chunks,)),
            dma((chunks,)),
            dma((chunks, PLANE)),
            dma((chunks, PLANE)),
            dma((PLANE,)),
            dma((PLANE,)),
            dma((nz,)),
            dma((nz,)),
        ],
        compiler_params=pltpu.CompilerParams(
            collective_id=0, has_side_effects=True, vmem_limit_bytes=VLIM),
        name="prefill",
    )(*[pltpu.with_memory_space_constraint(part_, pltpu.HBM) for part_ in (
        prompt_sizes, skip_gain, log_rates.reshape(1, head_count), packing,
        inputs, projections, step_sizes)])


def solution(mesh):
    in_specs = (
        P(None, ("groups", "ctx")),
        P(None, ("groups", "ctx")),
        P(None, ("groups", "ctx")),
        P(),
        P(),
        P(("groups", "ctx"), None),
        P("groups"),
    )
    out_specs = P(None, ("groups", "ctx"))
    return jax.shard_map(
        functools.partial(per_device, mesh.shape["ctx"]),
        mesh=mesh, in_specs=in_specs, out_specs=out_specs, check_vma=False,
    )
```

```python
import functools
import jax
import jax.numpy as jnp
from jax import lax
from jax.experimental import pallas as pl
from jax.experimental.pallas import tpu as pltpu
from jax.sharding import PartitionSpec as P

G = 4
BLOCK = 128
LANES = 128
PLANE = 4
LAGS = (1,2,4,5)
LAST_DONE = (7,6,4,3)
NEXT_DONE = (7, 6, 3, 2)
OUT_LAGS = (1,1,2,2)
VLIM = 36 * 1024 * 1024
F32 = jnp.float32
BF16 = jnp.bfloat16
MESH = pl.DeviceIdType.MESH


def dot_nt(a, b):
    return lax.dot_general(a, b, (((1,), (1,)), ((), ())), preferred_element_type=F32)


def starts_of(sizes_ref):
    out = []
    at = jnp.int32(0)
    for s in range(sizes_ref.shape[0]):
        out.append(at)
        at = at + sizes_ref[s]
    return out


def segment_of(position, starts):
    seg = jnp.zeros(position.shape, jnp.int32)
    for at in starts:
        seg = seg + (position >= at).astype(jnp.int32)
    return seg


def decay_of(dt, rate):
    t = dt.shape[0]
    tri = jnp.where(
        lax.broadcasted_iota(jnp.int32, (t, t), 0) >= lax.broadcasted_iota(jnp.int32, (t, t), 1),
        1.0, 0.0).astype(F32)
    return jnp.dot(tri, dt * rate, preferred_element_type=F32, precision=lax.Precision.HIGHEST)


def spread(value, heads, width):
    rows = value.shape[0]
    per = LANES // width
    lane = lax.broadcasted_iota(jnp.int32, (rows, LANES), 1)
    out = []
    for q in range(heads // per):
        acc = jnp.broadcast_to(value[:, q * per:q * per + 1], (rows, LANES))
        for k in range(1, per):
            other = jnp.broadcast_to(value[:, q * per + k:q * per + k + 1], (rows, LANES))
            acc = jnp.where(lane >= k * width, other, acc)
        out.append(acc)
    return jnp.concatenate(out, axis=1)


def fused_kernel(
    n, heads, width, states,
    sizes_hbm, skip_hbm, rate_hbm, pack_hbm, x_hbm, bc_hbm, dt_hbm, o_ref,
    sizes_ref, skip_ref, rate_ref, pack_ref, dt_ref,
    xv, bv, pick, ys, yr, ds, dr,
    cum_g, into_g, keep_g, cum_t, dt_t, opens, maps_t, gram, allow, acc,
    t_own, t0, t_in, enter, leave, out_e, carry, k_own, k_in, gains, p_own, p_in,
    in_sem, few_sem, ds_sem, dr_sem, ys_sem, yr_sem,
    ts_sem, tr_sem, es_sem, er_sem, cs_sem, cr_sem, ks_sem, kr_sem, ps_sem, pr_sem,
):
    me = lax.axis_index("ctx")
    tok = dt_ref.shape[1]
    slot = tok // n
    part = heads // 2
    wp = part * width
    wx = heads * width
    wm = 2 * states
    wq = wp // PLANE
    chunks = 2 * G
    blocks = tok // BLOCK
    half = n // 2
    q = lax.rem(me, PLANE)
    z = me // PLANE
    nz = n // PLANE
    base = me * tok

    def by_plane(values):
        return jnp.where(z == 0, values[0], jnp.where(
            z < nz // 2, values[1], jnp.where(z < nz - 1, values[2], values[3])))

    lag = by_plane(LAGS)

    def loop(count, body, low=0):
        def step(i, _):
            body(i)
            return 0
        lax.fori_loop(low, count, step, 0)

    def load_x(c):
        r = pl.ds(pl.multiple_of(c * wp, LANES), wp)
        return pltpu.make_async_copy(x_hbm.at[r], xv.at[c], in_sem.at[0, c])

    def load_m(g):
        r = pl.ds(pl.multiple_of(g * wm, LANES), wm)
        return pltpu.make_async_copy(bc_hbm.at[r], bv.at[g], in_sem.at[1, g])

    few = [
        pltpu.make_async_copy(src, dst, few_sem.at[i])
        for i, (src, dst) in enumerate((
            (pack_hbm, pack_ref), (dt_hbm, dt_ref), (sizes_hbm, sizes_ref),
            (skip_hbm, skip_ref), (rate_hbm, rate_ref)))
    ]
    few[0].start()
    few[1].start()
    load_m(0).start()
    load_x(0).start()
    load_x(1).start()

    barrier = pltpu.get_barrier_semaphore()
    loop(n, lambda off: pl.semaphore_signal(
        barrier, inc=1, device_id={"ctx": lax.rem(me + off, n)}, device_id_type=MESH), low=1)

    for copy in few[2:]:
        copy.start()
    loop(G, lambda g: load_m(g).start(), low=1)
    loop(chunks, lambda c: load_x(c).start(), low=2)
    few[0].wait()

    rows = lax.broadcasted_iota(jnp.int32, (tok, tok), 0)
    pick[...] = jnp.where(rows == pack_ref[...], 1.0, 0.0).astype(F32).T.astype(BF16)
    head_count = dt_ref.shape[0]
    few[1].wait()
    dt_all = dot_nt(pick[...], dt_ref[...]).astype(BF16)
    dt_all = jnp.concatenate([dt_all, jnp.zeros((tok, LANES - head_count), BF16)], axis=1)
    ds[...] = dt_all.reshape(n, slot, LANES)

    def lanes_of(k):
        return slice(0, wm + wp) if k == 0 else slice(wm + wp, wm + wx)

    def prep(g, k):
        if k == 0:
            load_m(g).wait()
            ys[g, :, :, :wm] = dot_nt(pick[...], bv[g]).astype(BF16).reshape(n, slot, wm)
        load_x(2 * g + k).wait()
        y = dot_nt(pick[...], xv[2 * g + k]).astype(BF16)
        ys[g, :, :, wm + k * wp:wm + (k + 1) * wp] = y.reshape(n, slot, wp)

    def send_y(g, k, off):
        to = lax.rem(me + off, n)
        s = lanes_of(k)
        return pltpu.make_async_remote_copy(
            ys.at[g, to, :, s], yr.at[g, me, :, s], ys_sem.at[g, k], yr_sem.at[g, k],
            device_id={"ctx": to}, device_id_type=MESH)

    def send_d(off):
        to = lax.rem(me + off, n)
        return pltpu.make_async_remote_copy(
            ds.at[to], dr.at[me], ds_sem.at[0], dr_sem.at[0],
            device_id={"ctx": to}, device_id_type=MESH)

    def spread_out(send):
        def pick_off(i):
            return 1 + lax.rem(2 * n - PLANE - 1 - i, n - 1)

        def tell(i, last):
            off = pick_off(i)
            there = lax.rem(me + off, n) // PLANE == nz - 1

            @pl.when(there if last else jnp.logical_not(there))
            def _():
                send(off).start()

        loop(n, lambda i: tell(i, False), low=1)
        loop(n, lambda i: tell(i, True), low=1)

    def issue(g, k):
        s = lanes_of(k)
        spread_out(lambda off: send_y(g, k, off))
        pltpu.make_async_copy(ys.at[g, me, :, s], yr.at[g, me, :, s], yr_sem.at[g, k]).start()

    def arrived(g, k):
        s = lanes_of(k)
        pltpu.make_async_copy(ys.at[g, :, :, s], yr.at[g, :, :, s], yr_sem.at[g, k]).wait()

    def departed(g, k):
        s = lanes_of(k)
        most = slice(0, n - 1)
        pltpu.make_async_copy(ys.at[g, most, :, s], yr.at[g, most, :, s], ys_sem.at[g, k]).wait()

    prep(0, 0)
    pl.semaphore_wait(barrier, n - 1)
    spread_out(send_d)
    pltpu.make_async_copy(ds.at[me], dr.at[me], dr_sem.at[0]).start()
    issue(0, 0)
    prep(0, 1)
    issue(0, 1)

    def prep_rest(g):
        prep(g, 0)
        prep(g, 1)

    loop(G, prep_rest, low=1)

    for copy in few[2:]:
        copy.wait()
    starts = starts_of(sizes_ref)
    rate = jnp.concatenate(
        [rate_ref[...], jnp.zeros((1, LANES - head_count), F32)], axis=1)
    rate = jnp.broadcast_to(-jnp.exp(rate), (8, LANES))[0:1]

    pltpu.make_async_copy(ds, dr, dr_sem.at[0]).wait()

    def rows_of(b):
        return slice(b * BLOCK // slot, (b + 1) * BLOCK // slot)

    for b in range(blocks):
        head = base + b * BLOCK
        last = head + BLOCK - 1
        dt = dr[rows_of(b)].reshape(BLOCK, LANES).astype(F32)
        cum = decay_of(dt, rate)
        end = cum[BLOCK - 1:BLOCK, :]
        pos = head + lax.broadcasted_iota(jnp.int32, (BLOCK, LANES), 0)
        last_seg = jnp.int32(0)
        cut = jnp.int32(0)
        for at in starts:
            last_seg = last_seg + (last >= at).astype(jnp.int32)
            cut = cut + ((at >= head) & (at <= last)).astype(jnp.int32)
        same = segment_of(pos, starts) == last_seg
        into = jnp.where(same, jnp.exp(end - cum), 0.0) * dt
        keep = jnp.broadcast_to(jnp.where(cut == 0, jnp.exp(end), 0.0), (8, LANES))
        for g in range(G):
            shift = (LANES - g * heads) % LANES
            cum_g[g, b] = pltpu.roll(cum, shift, 1)
            into_g[g, b] = pltpu.roll(into, shift, 1)
            keep_g[g, b] = pltpu.roll(keep, shift, 1)
        across = cum.T[:head_count]
        cum_t[b] = across
        dt_t[b] = dt.T[:head_count]
        row_pos = head + lax.broadcasted_iota(jnp.int32, (1, BLOCK), 1)
        row_cut = jnp.zeros((1, BLOCK), jnp.int32)
        for at in starts:
            row_cut = row_cut + ((row_pos >= at) & (at >= head)).astype(jnp.int32)
        opens[b] = jnp.where(row_cut == 0, jnp.exp(across), 0.0)
        pos_i = head + lax.broadcasted_iota(jnp.int32, (BLOCK, BLOCK), 0)
        pos_j = head + lax.broadcasted_iota(jnp.int32, (BLOCK, BLOCK), 1)
        fits = (pos_i >= pos_j) & (segment_of(pos_i, starts) == segment_of(pos_j, starts))
        allow[b] = jnp.where(fits, 0.0, -jnp.inf)

    for g in range(G):
        keep = keep_g[g, 0]
        for b in range(1, blocks):
            keep = keep * keep_g[g, b]
        k_own[g] = keep

    def send_keep(hop):
        return pltpu.make_async_remote_copy(
            k_own, k_in.at[q], ks_sem.at[hop], kr_sem.at[hop],
            device_id={"ctx": z * PLANE + lax.rem(q + hop, PLANE)}, device_id_type=MESH)

    own_keep = pltpu.make_async_copy(k_own, k_in.at[q], kr_sem.at[0])
    for hop in range(1, PLANE):
        send_keep(hop).start()
    own_keep.start()

    def y_of(g, b, lo, hi):
        return yr[g, rows_of(b), :, lo:hi].reshape(BLOCK, hi - lo)

    def x_of(g, k, b):
        return y_of(g, b, wm + k * wp, wm + (k + 1) * wp)

    def quarter(k):
        return slice(k * wq, (k + 1) * wq)

    def send_total(c, hop):
        to = lax.rem(q + hop, PLANE)
        s = pl.ds(pl.multiple_of(to * wq, LANES), wq)
        return pltpu.make_async_remote_copy(
            t_own.at[c, :, s], t_in.at[c, q], ts_sem.at[c, hop], tr_sem.at[c, hop],
            device_id={"ctx": z * PLANE + to}, device_id_type=MESH)

    def own_total(c):
        s = pl.ds(pl.multiple_of(q * wq, LANES), wq)
        return pltpu.make_async_copy(t_own.at[c, :, s], t_in.at[c, q], tr_sem.at[c, 0])

    def send_leave(c):
        return pltpu.make_async_remote_copy(
            leave.at[c], enter.at[c], es_sem.at[c], er_sem.at[c],
            device_id={"ctx": me + PLANE}, device_id_type=MESH)

    def take_enter(c):
        return pltpu.make_async_remote_copy(
            leave.at[c], enter.at[c], es_sem.at[c], er_sem.at[c],
            device_id={"ctx": me - PLANE}, device_id_type=MESH)

    def send_entering(c, hop):
        to = lax.rem(q + hop, PLANE)
        return pltpu.make_async_remote_copy(
            out_e.at[c, to], carry.at[c, q], cs_sem.at[c, hop], cr_sem.at[c, hop],
            device_id={"ctx": z * PLANE + to}, device_id_type=MESH)

    def own_entering(c):
        return pltpu.make_async_copy(out_e.at[c, q], carry.at[c, q], cr_sem.at[c, 0])

    def states_stage(g, k):
        c = 2 * g + k
        total = None
        for b in range(blocks):
            if k == 0:
                in_map = y_of(g, b, 0, states)
                out_map = y_of(g, b, states, wm)
                maps_t[b] = in_map.astype(F32).T.astype(BF16)
                gram[b] = dot_nt(out_map, in_map)
            cols = slice(k * part, (k + 1) * part)
            into = spread(into_g[g, b][:, cols], part, width)
            weighted = (x_of(g, k, b).astype(F32) * into).astype(BF16)
            block_total = jnp.dot(maps_t[b], weighted, preferred_element_type=F32)
            keep = spread(keep_g[g, b][:, cols], part, width)
            if total is None:
                total = block_total
            else:
                total = keep[0:1] * total + block_total
            if b < blocks - 1:
                t0[c, b, :states, :] = block_total
                t0[c, b, states:, :] = keep
        t_own[c] = total
        for hop in (2, 1, 3):
            send_total(c, hop).start()
        own_total(c).start()

    def inner_stage(g, k):
        c = 2 * g + k
        first = pl.multiple_of(c * part, part)
        for b in range(blocks):
            lo = b * BLOCK
            cum = cum_g[g, b]
            across = cum_t[b, pl.ds(first, part), :]
            dt = dt_t[b, pl.ds(first, part), :]
            x_fm = x_of(g, k, b).T
            for h in range(part):
                col = k * part + h
                gap = jnp.broadcast_to(cum[:, col:col + 1], (BLOCK, BLOCK)) - across[h:h + 1]
                mask = jnp.exp(gap + allow[b])
                mixing = (gram[b] * (mask * dt[h:h + 1])).astype(BF16)
                r = slice(h * width, (h + 1) * width)
                xh = x_fm[r]
                acc[c, r, lo:lo + BLOCK] = (
                    dot_nt(xh, mixing) + skip_ref[c * part + h] * xh.astype(F32))

    end = chunks - 1

    def totals_in(c):
        for hop in range(1, PLANE):
            send_total(c, hop).wait_recv()
        own_total(c).wait()

    def hand_out(c, state):
        for k in range(PLANE):
            out_e[c, k] = state
            if k < PLANE - 1:
                state = gains[c, k, 0:1] * state + t_in[c, k]
        for hop in (2, 1, 3):
            send_entering(c, hop).start()
        own_entering(c).start()

    def chain_stage(c):
        totals_in(c)

        @pl.when(z > 0)
        def _():
            take_enter(c).wait_recv()

        @pl.when(z == 0)
        def _():
            enter[c] = jnp.zeros((states, wq), F32)

        @pl.when(z < nz - 1)
        def _():
            state = enter[c]
            for k in range(PLANE):
                state = gains[c, k, 0:1] * state + t_in[c, k]
            leave[c] = state
            send_leave(c).start()

        hand_out(c, enter[c])

    def send_plane(to):
        return pltpu.make_async_remote_copy(
            p_own, p_in.at[z], ps_sem.at[to], pr_sem.at[z],
            device_id={"ctx": to * PLANE + q}, device_id_type=MESH)

    def take_plane(at):
        return pltpu.make_async_remote_copy(
            p_own, p_in.at[at], ps_sem.at[at], pr_sem.at[at],
            device_id={"ctx": at * PLANE + q}, device_id_type=MESH)

    told = jnp.where(z == 0, jnp.minimum(nz, 2), nz)

    def announce():
        totals_in(end)

        @pl.when(z < nz - 1)
        def _():
            total, gain = t_in[end, 0], gains[end, 0]
            for k in range(1, PLANE):
                total = gains[end, k, 0:1] * total + t_in[end, k]
                gain = gain * gains[end, k]
            p_own[:states] = total
            p_own[states:] = gain

            @pl.when(z == 1)
            def _():
                take_plane(0).wait_recv()
                p_own[:states] = gain[0:1] * p_in[0, :states] + total

            loop(told, lambda to: send_plane(to).start(), low=z + 1)

    def close_chain():
        enter[end] = jnp.zeros((states, wq), F32)

        def add(at):
            take_plane(at).wait_recv()
            enter[end] = p_in[at, states:states + 1] * enter[end] + p_in[at, :states]


        @pl.when(z == 1)
        def _():
            enter[end] = p_in[0, :states]

        loop(z, add, low=1)
        hand_out(end, enter[end])

    def output_stage(c):
        for hop in range(1, PLANE):
            send_entering(c, hop).wait_recv()
        own_entering(c).wait()
        g = c // 2
        first = pl.multiple_of(c * part, part)
        state = jnp.concatenate([carry[c, k] for k in range(PLANE)], axis=1)
        for b in range(blocks):
            lo = b * BLOCK
            out_map = y_of(g, b, states, wm)
            carried = dot_nt(state.astype(BF16).T, out_map)
            opened = opens[b, pl.ds(first, part), :]
            for h in range(part):
                r = slice(h * width, (h + 1) * width)
                o_ref[pl.ds(pl.multiple_of(c * wp + h * width, width), width), lo:lo + BLOCK] = (
                    acc[c, r, lo:lo + BLOCK] + carried[r] * opened[h:h + 1]).astype(BF16)
            if b < blocks - 1:
                state = t0[c, b, states:states + 1, :] * state + t0[c, b, :states, :]

    lane = lax.broadcasted_iota(jnp.int32, (8, wq), 1)

    def widen(c):
        first = lax.rem(c, 2) * part + q * (wq // width)
        for k in range(PLANE):
            keep = pltpu.roll(k_in[k, c // 2], lax.rem(LANES - first, LANES), 1)
            gain = jnp.broadcast_to(keep[:, 0:1], (8, wq))
            for h in range(1, wq // width):
                gain = jnp.where(lane >= h * width, jnp.broadcast_to(keep[:, h:h + 1], (8, wq)), gain)
            gains[c, k] = gain

    def done_by(step):
        due = jnp.maximum(step + 1 - lag, 0)
        due = jnp.where(step == end - 1, by_plane(NEXT_DONE), due)
        return jnp.where(step == end, by_plane(LAST_DONE), due)

    def follow(step):
        loop(done_by(step), chain_stage, low=done_by(step - 1))
        late = by_plane(OUT_LAGS)
        loop(done_by(step) - late, output_stage, low=jnp.maximum(done_by(step - 1) - late, 0))

    def turn(g):
        for k in range(2):
            arrived(g, k)

            @pl.when(g < G - 1)
            def _():
                issue(g + 1, k)

            states_stage(g, k)
            inner_stage(g, k)
            if k == 0:
                @pl.when(g == 0)
                def _():
                    own_keep.wait()
                    for hop in range(1, PLANE):
                        send_keep(hop).wait_recv()
                    loop(chunks, widen)

            follow(2 * g + k)

    loop(G, turn)
    done = by_plane(LAST_DONE)
    sent = done - by_plane(OUT_LAGS)
    early = jnp.maximum(sent, jnp.where(z == nz - 1, end - 4, 0))
    near = jnp.where(z < nz - 1, end, end - 1)
    loop(near, chain_stage, low=done)
    loop(early, output_stage, low=sent)
    announce()
    loop(end, chain_stage, low=near)
    close_chain()
    loop(chunks, output_stage, low=early)

    most = slice(0, n - 1)
    pltpu.make_async_copy(ds.at[most], dr.at[most], ds_sem.at[0]).wait()
    for hop in range(1, PLANE):
        send_keep(hop).wait_send()

    def close(g):
        for k in range(2):
            departed(g, k)
            c = 2 * g + k
            for hop in range(1, PLANE):
                send_total(c, hop).wait_send()
                send_entering(c, hop).wait_send()

            @pl.when((z < nz - 1) & (c < end))
            def _():
                send_leave(c).wait_send()


    loop(G, close)
    loop(told, lambda to: send_plane(to).wait_send(), low=z + 1)


def per_device(n, inputs, projections, step_sizes, log_rates, skip_gain, packing, prompt_sizes):
    tok = inputs.shape[1]
    head_count = log_rates.shape[0]
    heads = head_count // G
    states = projections.shape[0] // (2 * G)
    width = inputs.shape[0] // head_count
    part = heads // 2
    wp = part * width
    wx = heads * width
    wm = 2 * states
    wq = wp // PLANE
    slot = tok // n
    blocks = tok // BLOCK
    rows = states + 8
    nz = n // PLANE
    chunks = 2 * G
    hbm = pl.BlockSpec(memory_space=pltpu.HBM)
    dma = pltpu.SemaphoreType.DMA
    return pl.pallas_call(
        functools.partial(fused_kernel, n, heads, width, states),
        in_specs=[hbm] * 7,
        out_specs=pl.BlockSpec(memory_space=pltpu.VMEM),
        out_shape=jax.ShapeDtypeStruct((G * wx, tok), BF16),
        scratch_shapes=[
            pltpu.SMEM(prompt_sizes.shape, jnp.int32),
            pltpu.SMEM(skip_gain.shape, F32),
            pltpu.VMEM((1, head_count), F32),
            pltpu.VMEM((1, tok), jnp.int32),
            pltpu.VMEM((head_count, tok), BF16),
            pltpu.VMEM((chunks, wp, tok), BF16),
            pltpu.VMEM((G, wm, tok), BF16),
            pltpu.VMEM((tok, tok), BF16),
            pltpu.VMEM((G, n, slot, wm + wx), BF16),
            pltpu.VMEM((G, n, slot, wm + wx), BF16),
            pltpu.VMEM((n, slot, LANES), BF16),
            pltpu.VMEM((n, slot, LANES), BF16),
            pltpu.VMEM((G, blocks, BLOCK, LANES), F32),
            pltpu.VMEM((G, blocks, BLOCK, LANES), F32),
            pltpu.VMEM((G, blocks, 8, LANES), F32),
            pltpu.VMEM((blocks, head_count, BLOCK), F32),
            pltpu.VMEM((blocks, head_count, BLOCK), F32),
            pltpu.VMEM((blocks, head_count, BLOCK), F32),
            pltpu.VMEM((blocks, states, BLOCK), BF16),
            pltpu.VMEM((blocks, BLOCK, BLOCK), F32),
            pltpu.VMEM((blocks, BLOCK, BLOCK), F32),
            pltpu.VMEM((chunks, wp, tok), F32),
            pltpu.VMEM((chunks, states, wp), F32),
            pltpu.VMEM((chunks, blocks - 1, rows, wp), F32),
            pltpu.VMEM((chunks, PLANE, states, wq), F32),
            pltpu.VMEM((chunks, states, wq), F32),
            pltpu.VMEM((chunks, states, wq), F32),
            pltpu.VMEM((chunks, PLANE, states, wq), F32),
            pltpu.VMEM((chunks, PLANE, states, wq), F32),
            pltpu.VMEM((G, 8, LANES), F32),
            pltpu.VMEM((PLANE, G, 8, LANES), F32),
            pltpu.VMEM((chunks, PLANE, 8, wq), F32),
            pltpu.VMEM((states + 8, wq), F32),
            pltpu.VMEM((nz, states + 8, wq), F32),
            dma((2, chunks)),
            dma((5,)),
            dma((1,)),
            dma((1,)),
            dma((G, 2)),
            dma((G, 2)),
            dma((chunks, PLANE)),
            dma((chunks, PLANE)),
            dma((chunks,)),
            dma((chunks,)),
            dma((chunks, PLANE)),
            dma((chunks, PLANE)),
            dma((PLANE,)),
            dma((PLANE,)),
            dma((nz,)),
            dma((nz,)),
        ],
        compiler_params=pltpu.CompilerParams(
            collective_id=0, has_side_effects=True, vmem_limit_bytes=VLIM),
        name="prefill",
    )(*[pltpu.with_memory_space_constraint(part_, pltpu.HBM) for part_ in (
        prompt_sizes, skip_gain, log_rates.reshape(1, head_count), packing,
        inputs, projections, step_sizes)])


def solution(mesh):
    in_specs = (
        P(None, ("groups", "ctx")),
        P(None, ("groups", "ctx")),
        P(None, ("groups", "ctx")),
        P(),
        P(),
        P(("groups", "ctx"), None),
        P("groups"),
    )
    out_specs = P(None, ("groups", "ctx"))
    return jax.shard_map(
        functools.partial(per_device, mesh.shape["ctx"]),
        mesh=mesh, in_specs=in_specs, out_specs=out_specs, check_vma=False,
    )
```
